128 devices in a mesh: dp: 128 (over z, y, x, core).
Axes of the slice: x: 4, y: 4, z: 4, core: 2. Of those that a mesh axis runs over, the one named last changes fastest.
Arguments:
- queries: bfloat16 [8192, 2048], P('dp'), may hold values from -6 to 6
- new_kv: bfloat16 [2, 8192, 256], P(None, 'dp'), may hold values from -6 to 6
- residual: bfloat16 [8192, 2048], P('dp'), may hold values from -6 to 6
- prefix_cache: bfloat16 [2, 128, 1024, 256], P(None, 'dp'), may hold values from -6 to 6
- prefix_len: int32 [128], P('dp'), may hold values from 0 to 1024, as said below
- decode_cache: bfloat16 [2, 512, 1024, 256], P(None, 'dp'), may hold values from -6 to 6
- cache_len: int32 [512], P('dp'), may hold values from 1 to 1024, as said below
- placement: int32 [512], replicated, may hold values from 0 to 511, each once
- w_out: bfloat16 [2048, 2048], replicated, may hold values from -0.125 to 0.125
- norm_gain: bfloat16 [2048], replicated, may hold values from 0.099609375 to 1.8984375
- routes: int32 [8192, 8], P('dp'), may hold values from 0 to 127, all different within a row; in each aligned block of 64 rows (0 to 63, 64 to 127, ...) at most 8 rows name the same one
- route_weight: float32 [8192, 8], P('dp'), may hold values from 0.03 to 0.3
- w_gate: bfloat16 [128, 2048, 768], P('dp'), may hold values from -0.125 to 0.125
- w_up: bfloat16 [128, 2048, 768], P('dp'), may hold values from -0.125 to 0.125
- w_down: bfloat16 [128, 768, 2048], P('dp'), may hold values from -0.21875 to 0.21875
Outputs:
- mixed: bfloat16 [8192, 2048], P('dp')
The draws below stay inside these ranges and needn't reach their ends.
Inputs may be any that keep to these rules, and one draw needn't show every extreme that they name: `routes`: in the rows of one device (aligned blocks of 64 rows) no expert is named by more than 8 rows, a bound that some block reaches. `cache_len`: some slot holds 1024 cached tokens. `prefix_len`: some device's prefill request has 1024 earlier tokens. `placement`: every slot holds exactly one request.
All inputs are finite; a program needn't handle non-finite values.
Results may differ from the reference program's by a relative error of at most 0.014.
Values may be sent and summed in bfloat16 or wider, within the bound.
A program may use at most 128 MiB of HBM per device.

```python
import math
import jax
import jax.numpy as jnp
import numpy as np
from jax import lax

D = 2048
HEAD = 128
QHEADS = 16
KVHEADS = 2
FF = 768
TOPK = 8
STRETCH = 60
DEC_DEV = 4
CACHE = 1024
ROWS = 64
TOKENS = 8192
DECODES = 512
EXPERTS = 128
CAP = 8
QW = 2048
KW = 256
N_DP = 128


def draw_queries(key, part):
    values = jnp.clip(jax.random.normal(jax.random.fold_in(key, 1), (TOKENS, QW), jnp.float32), -6.0, 6.0)
    return values.astype(jnp.bfloat16)


def draw_new_kv(key, part):
    values = jnp.clip(jax.random.normal(jax.random.fold_in(key, 2), (2, TOKENS, KW), jnp.float32), -6.0, 6.0)
    return values.astype(jnp.bfloat16)


def draw_prefix_len(key, part):
    first_key, second_key = jax.random.split(jax.random.fold_in(key, 13))
    length = jax.random.randint(first_key, (N_DP,), 0, CACHE + 1)
    longest = jax.random.randint(second_key, (), 0, N_DP)
    return jnp.where(jnp.arange(N_DP, dtype=jnp.int32) == longest, CACHE, length).astype(jnp.int32)


def draw_cache_len(key, part):
    first_key, second_key, third_key = jax.random.split(jax.random.fold_in(key, 11), 3)
    exponent = jax.random.randint(first_key, (DECODES,), 0, 8)
    upper_span = jnp.maximum(jnp.right_shift(jnp.full((DECODES,), CACHE, jnp.int32), exponent), 1)
    length = 1 + jax.random.randint(second_key, (DECODES,), 0, 1 << 30) % upper_span
    longest = jax.random.randint(third_key, (), 0, DECODES)
    return jnp.where(jnp.arange(DECODES, dtype=jnp.int32) == longest, CACHE, length).astype(jnp.int32)


def block_levels(stream_key, shape, pieces, smallest, high):
    factor_of = 1.0
    for position, blocks in pieces:
        steps = jax.random.uniform(jax.random.fold_in(jax.random.fold_in(stream_key, 6), position), (blocks,), jnp.float32, smallest / len(pieces), high / len(pieces))
        factor_of = factor_of * jnp.repeat(jnp.exp(steps), shape[position] // blocks).reshape((-1,) + (1,) * (len(shape) - 1 - position))
    return factor_of


def deal_out(rng, own, number, rows, count, top, bound, slope):
    order = jax.random.permutation(rng, count)
    crowded, usual = portions_of(count, rows * top, bound, slope, True), portions_of(count, rows * top, bound, slope, False)
    places = jnp.arange(count)

    def named(sizes, turn):
        used = int((sizes > 0).sum())
        fixed = max(1, used // 4)
        shifted = fixed + (places - fixed + turn * (used - fixed)) % max(1, count - fixed)
        return jnp.zeros((count,), jnp.int32).at[order[jnp.where(places < fixed, places, shifted)]].set(jnp.asarray(sizes, jnp.int32))

    sizes = jnp.where(number % 4 == 0, named(crowded, number // 4), named(usual, number - number // 4 - 1))
    mixed = jax.random.permutation(jax.random.fold_in(own, 3), count)
    donor, taker = mixed[0:count // 2 * 2:2], mixed[1:count // 2 * 2:2]
    room = jnp.minimum(sizes[donor] - 1, bound - sizes[taker]) // 2
    room = jnp.where((donor == order[0]) | (taker == order[0]) | (sizes[taker] == 0), 0, jnp.maximum(room, 0))
    shifted = jax.random.randint(jax.random.fold_in(own, 4), (count // 2,), 0, 1 << 20) % (room + 1)
    sizes = sizes.at[donor].add(-shifted).at[taker].add(shifted)
    items = jnp.searchsorted(jnp.cumsum(sizes), jnp.arange(rows * top), side="right").astype(jnp.int32)
    grid = items.reshape(top, rows).T
    grid = grid[jax.random.permutation(jax.random.fold_in(own, 1), rows)]
    turn = jax.random.randint(jax.random.fold_in(own, 2), (rows, 1), 0, top)
    return jnp.take_along_axis(grid, (jnp.arange(top)[None, :] + turn) % top, axis=1)


def portions_of(number_of, total, most, lean, full):
    portions = [(1 << 20) // math.isqrt(rank ** lean) + 1 for rank in range(1, number_of + 1)]
    largest = most if full else min(most, max(-(-total // number_of), total * portions[0] // sum(portions)))
    least = 1 if total - largest >= number_of - 1 else 0
    holding, rest = [largest] + [least] * (number_of - 1), total - largest - least * (number_of - 1)
    while rest > 0:
        candidates = [i for i in range(1, number_of) if holding[i] < largest] or [i for i in range(1, number_of) if holding[i] < most]
        whole, remaining = sum([portions[i] for i in candidates]), rest
        for i in candidates:
            more = min(most - holding[i], max(1, remaining * portions[i] // whole), rest)
            holding[i] = holding[i] + more
            rest = rest - more
    return np.array(holding)


def centred(rng, dims, scale, bound, shards=(), kind=jnp.bfloat16):
    values = scale * jax.random.normal(rng, dims, jnp.float32)
    if shards:
        values = values * block_levels(rng, dims, shards, -0.22, 0.18)
    return jnp.clip(values, -bound, bound).astype(kind)


def setup_inputs(seed: int = 0) -> dict:
    splits = jax.random.split(jax.random.key(seed), 16)
    queries = draw_queries(jax.random.fold_in(splits[15], 71), 0)
    new_kv = draw_new_kv(jax.random.fold_in(splits[15], 71), 0)
    residual = centred(splits[2], (TOKENS, D), 1.0, 6.0, ((0, 128),))
    prefix_cache = centred(splits[3], (2, N_DP, CACHE, KW), 1.0, 6.0, ((1, 128),))
    prefix_len = draw_prefix_len(jax.random.fold_in(splits[15], 71), 0)
    decode_cache = centred(splits[5], (2, DECODES, CACHE, KW), 1.0, 6.0, ((1, 128),))
    cache_len = draw_cache_len(jax.random.fold_in(splits[15], 71), 0)
    placement = jax.random.permutation(splits[7], DECODES).astype(jnp.int32)
    w_out = centred(splits[8], (QW, D), QW ** -0.5, 0.125)
    norm_gain = jnp.clip(1.0 + 0.18 * jax.random.normal(splits[9], (D,), jnp.float32), 0.099609375, 1.8984375).astype(jnp.bfloat16)
    routes_keys = jax.random.split(jax.random.fold_in(splits[10], 1), TOKENS // ROWS)
    routes_turns = jax.random.permutation(jax.random.fold_in(splits[10], 3), TOKENS // ROWS)
    routes = jax.vmap(lambda own, number: deal_out(jax.random.fold_in(splits[10], 2), own, number, ROWS, EXPERTS, TOPK, CAP, 2))(routes_keys, routes_turns).reshape((TOKENS, TOPK))
    route_weight = jnp.clip(jnp.exp(math.log(0.3) - 2.3025852 * jax.random.uniform(splits[11], (TOKENS, TOPK), jnp.float32) ** block_levels(splits[11], (TOKENS, TOPK), ((0, 128),), -0.2, 0.2)), 0.03, 0.3)
    w_gate = centred(splits[12], (EXPERTS, D, FF), D ** -0.5, 0.125, ((0, 128),))
    w_up = centred(splits[13], (EXPERTS, D, FF), D ** -0.5, 0.125, ((0, 128),))
    w_down = centred(splits[14], (EXPERTS, FF, D), FF ** -0.5, 0.21875, ((0, 128),))
    return dict(queries=queries, new_kv=new_kv, residual=residual, prefix_cache=prefix_cache, prefix_len=prefix_len, decode_cache=decode_cache, cache_len=cache_len, placement=placement, w_out=w_out, norm_gain=norm_gain, routes=routes, route_weight=route_weight, w_gate=w_gate, w_up=w_up, w_down=w_down)


MASKED = -1e+30
EPSILON = 1e-06

def attend_sets(queries_in, key_sets):
    scale = 1.0 / math.sqrt(HEAD)
    scored = []
    for key_rows, value_rows, allowed in key_sets:
        raw = jnp.einsum('brkgd,blkd->brkgl', queries_in.astype(jnp.float32), key_rows.astype(jnp.float32)) * scale
        scored.append(jnp.where(allowed[:, :, None, None, :], raw, MASKED))
    highest = scored[0].max(axis=-1, keepdims=True)
    for entry in scored[1:]:
        highest = jnp.maximum(highest, entry.max(axis=-1, keepdims=True))
    exponent = [jnp.where(entry_set[2][:, :, None, None, :], jnp.exp(entry - highest), 0.0) for entry, entry_set in zip(scored, key_sets)]
    denominator = exponent[0].sum(axis=-1, keepdims=True)
    for entry in exponent[1:]:
        denominator = denominator + entry.sum(axis=-1, keepdims=True)
    result = None
    for entry, entry_set in zip(exponent, key_sets):
        probs = (entry / denominator).astype(jnp.bfloat16)
        piece = jnp.einsum('brkgl,blkd->brkgd', probs.astype(jnp.float32), entry_set[1].astype(jnp.float32))
        result = piece if result is None else result + piece
    return result.astype(jnp.bfloat16)

def reference(queries, new_kv, residual, prefix_cache, prefix_len, decode_cache, cache_len, placement, w_out, norm_gain, routes, route_weight, w_gate, w_up, w_down):
    group_size = QHEADS // KVHEADS
    blocks_q = queries.reshape(N_DP, ROWS, KVHEADS, group_size, HEAD)
    blocks_kv = new_kv.reshape(2, N_DP, ROWS, KVHEADS, HEAD)

    def prefill_block(device):
        query_rows = blocks_q[device][None, :STRETCH]
        prior = prefix_cache[:, device].reshape(2, 1, CACHE, KVHEADS, HEAD)
        fresh = blocks_kv[:, device, :STRETCH][:, None]
        positions = jnp.arange(CACHE, dtype=jnp.int32)
        earlier = jnp.broadcast_to(positions[None, None, :] < prefix_len[device], (1, STRETCH, CACHE))
        row_ids = jnp.arange(STRETCH, dtype=jnp.int32)
        causal = (row_ids[None, :] <= row_ids[:, None])[None]
        result = attend_sets(query_rows, [(prior[0], prior[1], earlier), (fresh[0], fresh[1], causal)])
        return result.reshape(STRETCH, QW)
    prefill_out = lax.map(prefill_block, jnp.arange(N_DP, dtype=jnp.int32))
    decode_query = blocks_q[:, STRETCH:].reshape(DECODES, 1, KVHEADS, group_size, HEAD)
    decode_pairs = blocks_kv[:, :, STRETCH:].reshape(2, DECODES, 1, KVHEADS, HEAD)
    chosen_cache = decode_cache[:, placement].reshape(2, DECODES, CACHE, KVHEADS, HEAD)
    lengths = cache_len[placement]
    positions = jnp.arange(CACHE, dtype=jnp.int32)
    cached_ok = (positions[None, :] < lengths[:, None])[:, None, :]
    own_ok = jnp.ones((DECODES, 1, 1), dtype=bool)
    decode_out = attend_sets(decode_query, [(chosen_cache[0], chosen_cache[1], cached_ok), (decode_pairs[0], decode_pairs[1], own_ok)])
    decode_out = decode_out.reshape(N_DP, DEC_DEV, QW)
    attended = jnp.concatenate([prefill_out, decode_out], axis=1).reshape(TOKENS, QW)
    hidden_state = (residual.astype(jnp.float32) + jnp.dot(attended, w_out, preferred_element_type=jnp.float32)).astype(jnp.bfloat16)
    hidden_f = hidden_state.astype(jnp.float32)
    normed = (hidden_f * lax.rsqrt(lax.optimization_barrier(jnp.mean(hidden_f * hidden_f, axis=-1, keepdims=True)) + EPSILON) * norm_gain.astype(jnp.float32)).astype(jnp.bfloat16)
    slot_total = N_DP * CAP

    def expert_step(carry, inputs):
        expert, gate_w, up_w, down_w = inputs
        chosen = routes == expert
        weight = lax.optimization_barrier(jnp.sum(jnp.where(chosen, route_weight, 0.0), axis=1))
        present = jnp.any(chosen, axis=1)
        index_rows = jnp.nonzero(present, size=slot_total, fill_value=0)[0].astype(jnp.int32)
        live = jnp.arange(slot_total, dtype=jnp.int32) < jnp.sum(present.astype(jnp.int32))
        taken = normed[index_rows].astype(jnp.float32)
        gate_part = jnp.dot(taken, gate_w.astype(jnp.float32), precision=lax.Precision.HIGHEST)
        up_part = jnp.dot(taken, up_w.astype(jnp.float32), precision=lax.Precision.HIGHEST)
        act = (jax.nn.silu(gate_part) * up_part).astype(jnp.bfloat16)
        result = jnp.dot(act.astype(jnp.float32), down_w.astype(jnp.float32), precision=lax.Precision.HIGHEST).astype(jnp.bfloat16)
        scaled = jnp.where(live[:, None], weight[index_rows][:, None] * result.astype(jnp.float32), 0.0)
        return (carry.at[index_rows].add(scaled), None)
    start = jnp.zeros((TOKENS, D), jnp.float32)
    expert_sum, _ = lax.scan(expert_step, start, (jnp.arange(EXPERTS, dtype=jnp.int32), w_gate, w_up, w_down))
    return (hidden_f + expert_sum).astype(jnp.bfloat16)
```

```python
import functools
import math

import jax
import jax.numpy as jnp
from jax import lax
from jax.experimental import pallas as pl
from jax.experimental.pallas import tpu as pltpu
from jax.sharding import PartitionSpec as P

HEAD = 128
MASKED = -1e30
EPSILON = 1e-06
MESH = pl.DeviceIdType.MESH
ORDERS = ((0, 1, 2), (1, 2, 0), (2, 0, 1))
STRIDES = (32, 8, 2)
DEC = 4
STRETCH = 60
GROUP = 8


def dot_t(a, b):
    return lax.dot_general(a, b, (((1,), (1,)), ((), ())), preferred_element_type=jnp.float32)


def dot_n(a, b):
    return lax.dot_general(a, b, (((1,), (0,)), ((), ())), preferred_element_type=jnp.float32)


class Gather:
    def __init__(self, me, sources, buffers, send_sem, recv_sem, local_sem):
        self.me = me
        self.coords = (me // 32, (me // 8) % 4, (me // 2) % 4)
        self.core = me % 2
        self.sources, self.buffers = sources, buffers
        self.send_sem, self.recv_sem, self.local_sem = send_sem, recv_sem, local_sem
        self.started = []

    def slot(self, buffer, gathered):
        index = tuple(
            slice(None) if axis in gathered else self.coords[axis] for axis in range(3)
        )
        return buffer.at[index + (self.core,)]

    def start(self, phase):
        started = []
        for p, (source, buffer) in enumerate(zip(self.sources, self.buffers)):
            order = ORDERS[p]
            if phase == 0:
                own = pltpu.make_async_copy(source, self.slot(buffer, ()), self.local_sem.at[p])
                own.start()
                started.append(own)
            if phase < 3:
                here = self.slot(buffer, order[:phase])
                axis = order[phase]
                for d in range(1, 4):
                    peer = self.me + ((self.coords[axis] + d) % 4 - self.coords[axis]) * STRIDES[axis]
                    copy = pltpu.make_async_remote_copy(
                        src_ref=source if phase == 0 else here,
                        dst_ref=here,
                        send_sem=self.send_sem.at[p, phase * 3 + d - 1],
                        recv_sem=self.recv_sem.at[p, phase * 3 + d - 1],
                        device_id=(peer,),
                        device_id_type=MESH,
                    )
                    copy.start()
                    started.append(copy)
            else:
                here = self.slot(buffer, (0, 1, 2))
                copy = pltpu.make_async_remote_copy(
                    src_ref=here,
                    dst_ref=here,
                    send_sem=self.send_sem.at[p, 9],
                    recv_sem=self.recv_sem.at[p, 9],
                    device_id=(self.me + 1 - 2 * self.core,),
                    device_id_type=MESH,
                )
                copy.start()
                started.append(copy)
        self.started = started

    def finish(self):
        for copy in self.started:
            copy.wait()
        self.started = []


def attention_kernel(
    index_ref, len_ref, q_ref, kv_ref, res_ref, gain_ref, q0_ref, q1_ref, pair_ref,
    prefix_hbm, cache_hbm, wout_hbm,
    hidden_ref, normed_ref,
    prefix, cache, wout, att, a0, a1, a2, b0, b1, s0, s1,
    load_sem, send_a, recv_a, local_a, send_b, recv_b, local_b,
):
    me = lax.axis_index("dp")
    loads = [
        pltpu.make_async_copy(prefix_hbm, prefix, load_sem.at[0]),
        pltpu.make_async_copy(cache_hbm, cache, load_sem.at[1]),
        pltpu.make_async_copy(wout_hbm, wout, load_sem.at[2]),
    ]
    for copy in loads:
        copy.start()
    first = Gather(me, (q0_ref, q1_ref, pair_ref), (a0, a1, a2), send_a, recv_a, local_a)
    second = Gather(me, (s0, s1), (b0, b1), send_b, recv_b, local_b)
    barrier = pltpu.get_barrier_semaphore()
    for axis in range(3):
        for d in range(1, 4):
            peer = me + ((first.coords[axis] + d) % 4 - first.coords[axis]) * STRIDES[axis]
            pl.semaphore_signal(barrier, inc=1, device_id=(peer,), device_id_type=MESH)
    pl.semaphore_signal(
        barrier, inc=1, device_id=(me + 1 - 2 * first.core,), device_id_type=MESH
    )
    pl.semaphore_wait(barrier, 10)
    scale = 1.0 / math.sqrt(HEAD)
    rows = q_ref.shape[0]
    cache_rows = prefix.shape[2 - 1]

    def prefill(part):
        g, half = part // 2, part % 2
        heads = [g * GROUP + half * 4 + j for j in range(4)]
        q = jnp.concatenate([q_ref[:, h * HEAD:(h + 1) * HEAD] for h in heads], axis=0)
        cols = slice(g * HEAD, (g + 1) * HEAD)
        old = dot_t(q, prefix[0, :, cols]) * scale
        new = dot_t(q, kv_ref[0, :, cols]) * scale
        position = lax.broadcasted_iota(jnp.int32, old.shape, 1)
        old = jnp.where(position < len_ref[DEC], old, MASKED)
        row = lax.broadcasted_iota(jnp.int32, new.shape, 0) % rows
        new = jnp.where(lax.broadcasted_iota(jnp.int32, new.shape, 1) <= row, new, MASKED)
        top = jnp.maximum(old.max(axis=-1, keepdims=True), new.max(axis=-1, keepdims=True))
        old, new = jnp.exp(old - top), jnp.exp(new - top)
        inv = 1.0 / (old.sum(axis=-1, keepdims=True) + new.sum(axis=-1, keepdims=True))
        out = dot_n((old * inv).astype(jnp.bfloat16), prefix[1, :, cols])
        out += dot_n((new * inv).astype(jnp.bfloat16), kv_ref[1, :, cols])
        for j, h in enumerate(heads):
            att[:, h * HEAD:(h + 1) * HEAD] = out[j * rows:(j + 1) * rows]

    first.start(0)
    loads[0].wait()
    prefill(0)
    first.finish()
    first.start(1)
    prefill(1)
    first.finish()
    first.start(2)
    prefill(2)
    first.finish()
    first.start(3)
    loads[1].wait()
    first.finish()

    for s in range(DEC):
        src = index_ref[s]
        sz, sy, sx, sc = src // 128, (src // 32) % 4, (src // 8) % 4, (src // 4) % 2
        sr = src % 4
        pair = a2[sz, sy, sx, sc, sr].astype(jnp.float32)
        for g, (buf, out_ref) in enumerate(((a0, s0), (a1, s1))):
            q = buf[sz, sy, sx, sc, sr]
            cols = slice(g * HEAD, (g + 1) * HEAD)
            old = dot_t(q, cache[0, s, :, cols]) * scale
            new = (q.astype(jnp.float32) * pair[g:g + 1]).sum(axis=-1, keepdims=True) * scale
            position = lax.broadcasted_iota(jnp.int32, old.shape, 1)
            old = jnp.where(position < len_ref[s], old, MASKED)
            top = jnp.maximum(old.max(axis=-1, keepdims=True), new)
            old, new = jnp.exp(old - top), jnp.exp(new - top)
            inv = 1.0 / (old.sum(axis=-1, keepdims=True) + new)
            out = dot_n((old * inv).astype(jnp.bfloat16), cache[1, s, :, cols])
            own = (new * inv).astype(jnp.bfloat16).astype(jnp.float32)
            out_ref[s] = (out + own * pair[2 + g:3 + g]).astype(jnp.bfloat16)

    second.start(0)
    prefill(3)
    second.finish()
    second.start(1)
    loads[2].wait()
    second.finish()
    second.start(2)
    second.finish()
    second.start(3)
    second.finish()
    for s in range(DEC):
        src = index_ref[DEC + s]
        sz, sy, sx, sc = src // 128, (src // 32) % 4, (src // 8) % 4, (src // 4) % 2
        sr = src % 4
        for g, buf in enumerate((b0, b1)):
            out = buf[sz, sy, sx, sc, sr].astype(jnp.float32)
            for j in range(GROUP):
                h = g * GROUP + j
                att[STRETCH + s:STRETCH + s + 1, h * HEAD:(h + 1) * HEAD] = out[j:j + 1]

    attended = att[...].astype(jnp.bfloat16)
    step = 512
    total = jnp.zeros((rows, 1), jnp.float32)
    width = wout.shape[1]
    for n in range(0, width, step):
        piece = dot_n(attended, wout[:, n:n + step])
        piece = (piece + res_ref[:, n:n + step].astype(jnp.float32)).astype(jnp.bfloat16)
        hidden_ref[:, n:n + step] = piece
        piece = piece.astype(jnp.float32)
        total += (piece * piece).sum(axis=-1, keepdims=True)
    norm = lax.rsqrt(total * (1.0 / width) + EPSILON)
    normed_ref[...] = (
        hidden_ref[...].astype(jnp.float32) * norm * gain_ref[...].astype(jnp.float32)
    ).astype(jnp.bfloat16)


def attention(index, lens, queries, new_kv, residual, gain, q0, q1, pair, prefix, cache, w_out):
    rows, width = residual.shape
    vmem = pl.BlockSpec(memory_space=pltpu.VMEM)
    smem = pl.BlockSpec(memory_space=pltpu.SMEM)
    hbm = pl.BlockSpec(memory_space=pl.ANY)
    bf16 = jnp.bfloat16
    dma = pltpu.SemaphoreType.DMA
    return pl.pallas_call(
        attention_kernel,
        out_shape=[jax.ShapeDtypeStruct((rows, width), bf16)] * 2,
        in_specs=[smem, smem] + [vmem] * 7 + [hbm] * 3,
        out_specs=[vmem, vmem],
        scratch_shapes=[
            pltpu.VMEM(prefix.shape, bf16),
            pltpu.VMEM(cache.shape, bf16),
            pltpu.VMEM(w_out.shape, bf16),
            pltpu.VMEM((rows, queries.shape[1]), jnp.float32),
            pltpu.VMEM((4, 4, 4, 2) + q0.shape, bf16),
            pltpu.VMEM((4, 4, 4, 2) + q1.shape, bf16),
            pltpu.VMEM((4, 4, 4, 2) + pair.shape, bf16),
            pltpu.VMEM((4, 4, 4, 2) + q0.shape, bf16),
            pltpu.VMEM((4, 4, 4, 2) + q1.shape, bf16),
            pltpu.VMEM(q0.shape, bf16),
            pltpu.VMEM(q1.shape, bf16),
            dma((3,)),
            dma((3, 10)), dma((3, 10)), dma((3,)),
            dma((2, 10)), dma((2, 10)), dma((2,)),
        ],
        compiler_params=pltpu.CompilerParams(
            collective_id=0, has_side_effects=True, vmem_limit_bytes=56 * 2**20
        ),
        name="attention",
    )(index, lens, queries, new_kv, residual, gain, q0, q1, pair, prefix, cache, w_out)


def expert_rows(block, gate_w, up_w, down_w):
    block_shape = block.shape
    flat_rows = block.reshape(-1, block_shape[-1])
    gate_part = jnp.dot(flat_rows, gate_w[0], preferred_element_type=jnp.float32)
    up_part = jnp.dot(flat_rows, up_w[0], preferred_element_type=jnp.float32)
    act = (jax.nn.silu(gate_part) * up_part).astype(jnp.bfloat16)
    result = jnp.dot(act, down_w[0], preferred_element_type=jnp.float32).astype(jnp.bfloat16)
    return result.reshape(block_shape)


def local(
    queries, new_kv, residual, prefix_cache, prefix_len, decode_cache, cache_len, placement,
    w_out, norm_gain, routes, route_weight, w_gate, w_up, w_down,
):
    row_count, width = residual.shape
    experts = lax.axis_size("dp")
    capacity = max(2, 2 * row_count * routes.shape[1] // experts)
    me = lax.axis_index("dp")
    slot_ids = me * DEC + jnp.arange(DEC, dtype=jnp.int32)
    request_ids = jnp.arange(placement.shape[0], dtype=jnp.int32)
    matches = placement[None, :] == slot_ids[:, None]
    request = jnp.sum(jnp.where(matches, request_ids[None, :], 0), axis=1)
    my_slots = lax.dynamic_slice_in_dim(placement, me * DEC, DEC)
    index = jnp.concatenate([request, my_slots])
    lens = jnp.concatenate([cache_len, prefix_len])
    q = queries[STRETCH:].reshape(DEC, 2, GROUP, HEAD)
    pair = jnp.transpose(new_kv[:, STRETCH:].reshape(2, DEC, 2, HEAD), (1, 0, 2, 3))
    pair = pair.reshape(DEC, 4, HEAD)
    hidden_state, normed = attention(
        index, lens, queries, new_kv, residual, norm_gain.reshape(1, width), q[:, 0], q[:, 1], pair,
        prefix_cache[:, 0], decode_cache, w_out,
    )
    expert_ids = jnp.arange(experts, dtype=jnp.int32)
    named = routes[:, :, None] == expert_ids[None, None, :]
    member = jnp.any(named, axis=1)
    weight = jnp.sum(jnp.where(named, route_weight[:, :, None], 0.0), axis=1)
    row_ids = jnp.arange(row_count, dtype=jnp.int32)
    lower = (row_ids[None, :] < row_ids[:, None]).astype(jnp.bfloat16)
    rank = jnp.dot(lower, member.astype(jnp.bfloat16), preferred_element_type=jnp.float32)
    rank = jnp.where(member, rank, -1.0).T
    slots = jnp.arange(capacity, dtype=jnp.float32)
    chosen = rank[:, None, :] == slots[None, :, None]
    picks = chosen.reshape(experts * capacity, row_count)
    buffer = jnp.dot(picks.astype(jnp.bfloat16), normed, preferred_element_type=jnp.float32)
    buffer = buffer.astype(jnp.bfloat16).reshape(experts, capacity, width)
    arrived_rows = lax.all_to_all(buffer, "dp", split_axis=0, concat_axis=0, tiled=True)
    served = expert_rows(arrived_rows, w_gate, w_up, w_down)
    returned = lax.all_to_all(served, "dp", split_axis=0, concat_axis=0, tiled=True)
    mix = jnp.where(chosen, weight.T[:, None, :], 0.0).reshape(experts * capacity, row_count)
    high = lax.reduce_precision(mix, 8, 7)
    rest = (mix - high).astype(jnp.bfloat16)
    both = jnp.concatenate([high.astype(jnp.bfloat16), rest], axis=1)
    sums = lax.dot_general(
        both, returned.reshape(experts * capacity, width), (((0,), (0,)), ((), ())),
        preferred_element_type=jnp.float32,
    )
    mixed = hidden_state.astype(jnp.float32) + sums[:row_count] + sums[row_count:]
    return mixed.astype(jnp.bfloat16)


def solution(mesh):
    in_specs = (
        P("dp", None),
        P(None, "dp", None),
        P("dp", None),
        P(None, "dp", None, None),
        P("dp"),
        P(None, "dp", None, None),
        P("dp"),
        P(),
        P(),
        P(),
        P("dp", None),
        P("dp", None),
        P("dp", None, None),
        P("dp", None, None),
        P("dp", None, None),
    )
    out_specs = P("dp", None)
    return jax.shard_map(local, mesh=mesh, in_specs=in_specs, out_specs=out_specs, check_vma=False)
```

```python
import functools
import math

import jax
import jax.numpy as jnp
from jax import lax
from jax.experimental import pallas as pl
from jax.experimental.pallas import tpu as pltpu
from jax.sharding import PartitionSpec as P

HEAD = 128
MASKED = -1e30
EPSILON = 1e-06
MESH = pl.DeviceIdType.MESH
ORDERS = ((0, 1, 2), (1, 2, 0), (2, 0, 1))
STRIDES = (32, 8, 2)
DEC = 4
STRETCH = 60
GROUP = 8


def dot_t(a, b):
    return lax.dot_general(a, b, (((1,), (1,)), ((), ())), preferred_element_type=jnp.float32)


def dot_n(a, b):
    return lax.dot_general(a, b, (((1,), (0,)), ((), ())), preferred_element_type=jnp.float32)


class Gather:
    def __init__(self, me, sources, buffers, send_sem, recv_sem, local_sem):
        self.me = me
        self.coords = (me // 32, (me // 8) % 4, (me // 2) % 4)
        self.core = me % 2
        self.sources, self.buffers = sources, buffers
        self.send_sem, self.recv_sem, self.local_sem = send_sem, recv_sem, local_sem
        self.started = []

    def slot(self, buffer, gathered):
        index = tuple(
            slice(None) if axis in gathered else self.coords[axis] for axis in range(3)
        )
        return buffer.at[index + (self.core,)]

    def start(self, phase):
        started = []
        for p, (source, buffer) in enumerate(zip(self.sources, self.buffers)):
            order = ORDERS[p]
            if phase == 0:
                own = pltpu.make_async_copy(source, self.slot(buffer, ()), self.local_sem.at[p])
                own.start()
                started.append(own)
            if phase < 3:
                here = self.slot(buffer, order[:phase])
                axis = order[phase]
                for d in range(1, 4):
                    peer = self.me + ((self.coords[axis] + d) % 4 - self.coords[axis]) * STRIDES[axis]
                    copy = pltpu.make_async_remote_copy(
                        src_ref=source if phase == 0 else here,
                        dst_ref=here,
                        send_sem=self.send_sem.at[p, phase * 3 + d - 1],
                        recv_sem=self.recv_sem.at[p, phase * 3 + d - 1],
                        device_id=(peer,),
                        device_id_type=MESH,
                    )
                    copy.start()
                    started.append(copy)
            else:
                here = self.slot(buffer, (0, 1, 2))
                copy = pltpu.make_async_remote_copy(
                    src_ref=here,
                    dst_ref=here,
                    send_sem=self.send_sem.at[p, 9],
                    recv_sem=self.recv_sem.at[p, 9],
                    device_id=(self.me + 1 - 2 * self.core,),
                    device_id_type=MESH,
                )
                copy.start()
                started.append(copy)
        self.started = started

    def finish(self):
        for copy in self.started:
            copy.wait()
        self.started = []


def attention_kernel(
    index_ref, len_ref, q_ref, kv_ref, res_ref, gain_ref, q0_ref, q1_ref, pair_ref,
    prefix_hbm, cache_hbm, wout_hbm,
    hidden_ref, normed_ref,
    prefix, cache, wout, att, a0, a1, a2, b0, b1, s0, s1,
    load_sem, send_a, recv_a, local_a, send_b, recv_b, local_b,
):
    me = lax.axis_index("dp")
    loads = [
        pltpu.make_async_copy(prefix_hbm, prefix, load_sem.at[0]),
        pltpu.make_async_copy(cache_hbm, cache, load_sem.at[1]),
        pltpu.make_async_copy(wout_hbm, wout, load_sem.at[2]),
    ]
    for copy in loads:
        copy.start()
    first = Gather(me, (q0_ref, q1_ref, pair_ref), (a0, a1, a2), send_a, recv_a, local_a)
    second = Gather(me, (s0, s1), (b0, b1), send_b, recv_b, local_b)
    barrier = pltpu.get_barrier_semaphore()
    for axis in range(3):
        for d in range(1, 4):
            peer = me + ((first.coords[axis] + d) % 4 - first.coords[axis]) * STRIDES[axis]
            pl.semaphore_signal(barrier, inc=1, device_id=(peer,), device_id_type=MESH)
    pl.semaphore_signal(
        barrier, inc=1, device_id=(me + 1 - 2 * first.core,), device_id_type=MESH
    )
    pl.semaphore_wait(barrier, 10)
    scale = 1.0 / math.sqrt(HEAD)
    rows = q_ref.shape[0]
    cache_rows = prefix.shape[2 - 1]

    def prefill(part):
        g, half = part // 2, part % 2
        heads = [g * GROUP + half * 4 + j for j in range(4)]
        q = jnp.concatenate([q_ref[:, h * HEAD:(h + 1) * HEAD] for h in heads], axis=0)
        cols = slice(g * HEAD, (g + 1) * HEAD)
        old = dot_t(q, prefix[0, :, cols]) * scale
        new = dot_t(q, kv_ref[0, :, cols]) * scale
        position = lax.broadcasted_iota(jnp.int32, old.shape, 1)
        old = jnp.where(position < len_ref[DEC], old, MASKED)
        row = lax.broadcasted_iota(jnp.int32, new.shape, 0) % rows
        new = jnp.where(lax.broadcasted_iota(jnp.int32, new.shape, 1) <= row, new, MASKED)
        top = jnp.maximum(old.max(axis=-1, keepdims=True), new.max(axis=-1, keepdims=True))
        old, new = jnp.exp(old - top), jnp.exp(new - top)
        inv = 1.0 / (old.sum(axis=-1, keepdims=True) + new.sum(axis=-1, keepdims=True))
        out = dot_n((old * inv).astype(jnp.bfloat16), prefix[1, :, cols])
        out += dot_n((new * inv).astype(jnp.bfloat16), kv_ref[1, :, cols])
        for j, h in enumerate(heads):
            att[:, h * HEAD:(h + 1) * HEAD] = out[j * rows:(j + 1) * rows]

    first.start(0)
    loads[0].wait()
    prefill(0)
    first.finish()
    first.start(1)
    prefill(1)
    first.finish()
    first.start(2)
    prefill(2)
    first.finish()
    first.start(3)
    loads[1].wait()
    first.finish()

    for s in range(DEC):
        src = index_ref[s]
        sz, sy, sx, sc = src // 128, (src // 32) % 4, (src // 8) % 4, (src // 4) % 2
        sr = src % 4
        pair = a2[sz, sy, sx, sc, sr].astype(jnp.float32)
        for g, (buf, out_ref) in enumerate(((a0, s0), (a1, s1))):
            q = buf[sz, sy, sx, sc, sr]
            cols = slice(g * HEAD, (g + 1) * HEAD)
            old = dot_t(q, cache[0, s, :, cols]) * scale
            new = (q.astype(jnp.float32) * pair[g:g + 1]).sum(axis=-1, keepdims=True) * scale
            position = lax.broadcasted_iota(jnp.int32, old.shape, 1)
            old = jnp.where(position < len_ref[s], old, MASKED)
            top = jnp.maximum(old.max(axis=-1, keepdims=True), new)
            old, new = jnp.exp(old - top), jnp.exp(new - top)
            inv = 1.0 / (old.sum(axis=-1, keepdims=True) + new)
            out = dot_n((old * inv).astype(jnp.bfloat16), cache[1, s, :, cols])
            own = (new * inv).astype(jnp.bfloat16).astype(jnp.float32)
            out_ref[s] = (out + own * pair[2 + g:3 + g]).astype(jnp.bfloat16)

    second.start(0)
    prefill(3)
    second.finish()
    second.start(1)
    loads[2].wait()
    second.finish()
    second.start(2)
    second.finish()
    second.start(3)
    second.finish()
    for s in range(DEC):
        src = index_ref[DEC + s]
        sz, sy, sx, sc = src // 128, (src // 32) % 4, (src // 8) % 4, (src // 4) % 2
        sr = src % 4
        for g, buf in enumerate((b0, b1)):
            out = buf[sz, sy, sx, sc, sr].astype(jnp.float32)
            for j in range(GROUP):
                h = g * GROUP + j
                att[STRETCH + s:STRETCH + s + 1, h * HEAD:(h + 1) * HEAD] = out[j:j + 1]

    attended = att[...].astype(jnp.bfloat16)
    step = 512
    total = jnp.zeros((rows, 1), jnp.float32)
    width = wout.shape[1]
    for n in range(0, width, step):
        piece = dot_n(attended, wout[:, n:n + step])
        piece = (piece + res_ref[:, n:n + step].astype(jnp.float32)).astype(jnp.bfloat16)
        hidden_ref[:, n:n + step] = piece
        piece = piece.astype(jnp.float32)
        total += (piece * piece).sum(axis=-1, keepdims=True)
    norm = lax.rsqrt(total * (1.0 / width) + EPSILON)
    normed_ref[...] = (
        hidden_ref[...].astype(jnp.float32) * norm * gain_ref[...].astype(jnp.float32)
    ).astype(jnp.bfloat16)


def attention(index, lens, queries, new_kv, residual, gain, q0, q1, pair, prefix, cache, w_out):
    rows, width = residual.shape
    vmem = pl.BlockSpec(memory_space=pltpu.VMEM)
    smem = pl.BlockSpec(memory_space=pltpu.SMEM)
    hbm = pl.BlockSpec(memory_space=pl.ANY)
    bf16 = jnp.bfloat16
    dma = pltpu.SemaphoreType.DMA
    return pl.pallas_call(
        attention_kernel,
        out_shape=[jax.ShapeDtypeStruct((rows, width), bf16)] * 2,
        in_specs=[smem, smem] + [vmem] * 7 + [hbm] * 3,
        out_specs=[vmem, vmem],
        scratch_shapes=[
            pltpu.VMEM(prefix.shape, bf16),
            pltpu.VMEM(cache.shape, bf16),
            pltpu.VMEM(w_out.shape, bf16),
            pltpu.VMEM((rows, queries.shape[1]), jnp.float32),
            pltpu.VMEM((4, 4, 4, 2) + q0.shape, bf16),
            pltpu.VMEM((4, 4, 4, 2) + q1.shape, bf16),
            pltpu.VMEM((4, 4, 4, 2) + pair.shape, bf16),
            pltpu.VMEM((4, 4, 4, 2) + q0.shape, bf16),
            pltpu.VMEM((4, 4, 4, 2) + q1.shape, bf16),
            pltpu.VMEM(q0.shape, bf16),
            pltpu.VMEM(q1.shape, bf16),
            dma((3,)),
            dma((3, 10)), dma((3, 10)), dma((3,)),
            dma((2, 10)), dma((2, 10)), dma((2,)),
        ],
        compiler_params=pltpu.CompilerParams(
            collective_id=0, has_side_effects=True, vmem_limit_bytes=56 * 2**20
        ),
        name="attention",
    )(index, lens, queries, new_kv, residual, gain, q0, q1, pair, prefix, cache, w_out)


def shifted(me, k, i, sign):
    dx, dy, dc = i % 4, (i // 4) % 4, i // 16
    dz = (dx + dy + k) % 4
    z = (me // 32 + 4 + sign * dz) % 4
    y = ((me // 8) % 4 + 4 + sign * dy) % 4
    x = ((me // 2) % 4 + 4 + sign * dx) % 4
    return z * 32 + y * 8 + x * 2 + (me + dc) % 2


def experts_kernel(
    picks_ref, mix_ref, normed_ref, hidden_ref, gate_hbm, up_hbm, down_hbm,
    out_ref,
    gate, up, down, outgoing, arrived, served, returned,
    load_sem, local_sem, send_out, recv_out, send_back, recv_back,
):
    me = lax.axis_index("dp")
    loads = [
        pltpu.make_async_copy(source.at[0], target, load_sem.at[n])
        for n, (source, target) in enumerate(((gate_hbm, gate), (up_hbm, up), (down_hbm, down)))
    ]
    for copy in loads:
        copy.start()
    barrier = pltpu.get_barrier_semaphore()
    groups, members, capacity, width = outgoing.shape
    count = members * capacity
    low = lambda k: 1 if k == 0 else 0

    for k in range(groups):
        def greet(i, carry, k=k):
            pl.semaphore_signal(
                barrier, inc=1, device_id=(shifted(me, k, i, 1),), device_id_type=MESH
            )
            return carry

        lax.fori_loop(low(k), members, greet, 0)
    for k in range(groups):
        block = dot_n(picks_ref[k * count:(k + 1) * count], normed_ref[...])
        outgoing[k] = block.astype(jnp.bfloat16).reshape(members, capacity, width)
    pl.semaphore_wait(barrier, groups * members - 1)

    def transfer(source, target, send_sem, recv_sem, k, part, peer):
        return pltpu.make_async_remote_copy(
            src_ref=source.at[k, part], dst_ref=target.at[k, part],
            send_sem=send_sem.at[k], recv_sem=recv_sem.at[k],
            device_id=(peer,), device_id_type=MESH,
        )

    def send(source, target, send_sem, recv_sem, k, sign):
        def one(i, carry):
            transfer(
                source, target, send_sem, recv_sem, k, i, shifted(me, k, i, sign)
            ).start()
            return carry

        lax.fori_loop(low(k), members, one, 0)

    def whole(source, target, send_sem, recv_sem, k):
        part = pl.ds(low(k), members - low(k))
        return transfer(source, target, send_sem, recv_sem, k, part, shifted(me, k, 1, 1))

    out_args = (outgoing, arrived, send_out, recv_out)
    back_args = (served, returned, send_back, recv_back)
    own_out = pltpu.make_async_copy(outgoing.at[0, 0], arrived.at[0, 0], local_sem.at[0])
    own_back = pltpu.make_async_copy(served.at[0, 0], returned.at[0, 0], local_sem.at[1])
    own_out.start()
    for k in range(groups):
        send(*out_args, k, 1)
    for copy in loads:
        copy.wait()
    own_out.wait()
    for k in range(groups):
        whole(*out_args, k).wait_recv()
        rows = arrived[k].reshape(count, width)
        gate_part = dot_n(rows, gate[...])
        act = gate_part / (1.0 + jnp.exp(-gate_part)) * dot_n(rows, up[...])
        result = dot_n(act.astype(jnp.bfloat16), down[...])
        served[k] = result.astype(jnp.bfloat16).reshape(members, capacity, width)
        if k == 0:
            own_back.start()
        send(*back_args, k, -1)
    own_back.wait()
    total = None
    for k in range(groups):
        whole(*back_args, k).wait_recv()
        part = dot_n(mix_ref[:, k * count:(k + 1) * count], returned[k].reshape(count, width))
        total = part if total is None else total + part
    tokens = hidden_ref.shape[0]
    out_ref[...] = (
        hidden_ref[...].astype(jnp.float32) + total[:tokens] + total[tokens:]
    ).astype(jnp.bfloat16)
    for k in range(groups):
        whole(*out_args, k).wait_send()
        whole(*back_args, k).wait_send()


def routed_experts(picks, mix, normed, hidden, w_gate, w_up, w_down):
    tokens, width = hidden.shape
    vmem = pl.BlockSpec(memory_space=pltpu.VMEM)
    hbm = pl.BlockSpec(memory_space=pl.ANY)
    bf16 = jnp.bfloat16
    dma = pltpu.SemaphoreType.DMA
    slots = pltpu.VMEM((4, 32, picks.shape[0] // 128, width), bf16)
    return pl.pallas_call(
        experts_kernel,
        out_shape=jax.ShapeDtypeStruct((tokens, width), bf16),
        in_specs=[vmem] * 4 + [hbm] * 3,
        out_specs=vmem,
        scratch_shapes=[
            pltpu.VMEM(w_gate.shape[1:], bf16),
            pltpu.VMEM(w_up.shape[1:], bf16),
            pltpu.VMEM(w_down.shape[1:], bf16),
            slots, slots, slots, slots,
            dma((3,)), dma((2,)), dma((4,)), dma((4,)), dma((4,)), dma((4,)),
        ],
        compiler_params=pltpu.CompilerParams(
            collective_id=1, has_side_effects=True, vmem_limit_bytes=56 * 2**20
        ),
        name="experts",
    )(picks, mix, normed, hidden, w_gate, w_up, w_down)


def local(
    queries, new_kv, residual, prefix_cache, prefix_len, decode_cache, cache_len, placement,
    w_out, norm_gain, routes, route_weight, w_gate, w_up, w_down,
):
    row_count, width = residual.shape
    experts = lax.axis_size("dp")
    capacity = max(2, 2 * row_count * routes.shape[1] // experts)
    me = lax.axis_index("dp")
    slot_ids = me * DEC + jnp.arange(DEC, dtype=jnp.int32)
    request_ids = jnp.arange(placement.shape[0], dtype=jnp.int32)
    matches = placement[None, :] == slot_ids[:, None]
    request = jnp.sum(jnp.where(matches, request_ids[None, :], 0), axis=1)
    my_slots = lax.dynamic_slice_in_dim(placement, me * DEC, DEC)
    index = jnp.concatenate([request, my_slots])
    lens = jnp.concatenate([cache_len, prefix_len])
    q = queries[STRETCH:].reshape(DEC, 2, GROUP, HEAD)
    pair = jnp.transpose(new_kv[:, STRETCH:].reshape(2, DEC, 2, HEAD), (1, 0, 2, 3))
    pair = pair.reshape(DEC, 4, HEAD)
    hidden_state, normed = attention(
        index, lens, queries, new_kv, residual, norm_gain.reshape(1, width), q[:, 0], q[:, 1], pair,
        prefix_cache[:, 0], decode_cache, w_out,
    )
    numbers = jnp.arange(experts, dtype=jnp.int32)
    expert_ids = shifted(me, numbers // 32, numbers % 32, 1)
    named = routes[:, :, None] == expert_ids[None, None, :]
    member = jnp.any(named, axis=1)
    weight = jnp.sum(jnp.where(named, route_weight[:, :, None], 0.0), axis=1)
    row_ids = jnp.arange(row_count, dtype=jnp.int32)
    lower = (row_ids[None, :] < row_ids[:, None]).astype(jnp.bfloat16)
    rank = jnp.dot(lower, member.astype(jnp.bfloat16), preferred_element_type=jnp.float32)
    rank = jnp.where(member, rank, -1.0).T
    slots = jnp.arange(capacity, dtype=jnp.float32)
    chosen = rank[:, None, :] == slots[None, :, None]
    picks = chosen.reshape(experts * capacity, row_count).astype(jnp.bfloat16)
    mix = jnp.where(chosen, weight.T[:, None, :], 0.0).reshape(experts * capacity, row_count).T
    high = lax.reduce_precision(mix, 8, 7)
    rest = (mix - high).astype(jnp.bfloat16)
    both = jnp.concatenate([high.astype(jnp.bfloat16), rest], axis=0)
    return routed_experts(picks, both, normed, hidden_state, w_gate, w_up, w_down)


def solution(mesh):
    in_specs = (
        P("dp", None),
        P(None, "dp", None),
        P("dp", None),
        P(None, "dp", None, None),
        P("dp"),
        P(None, "dp", None, None),
        P("dp"),
        P(),
        P(),
        P(),
        P("dp", None),
        P("dp", None),
        P("dp", None, None),
        P("dp", None, None),
        P("dp", None, None),
    )
    out_specs = P("dp", None)
    return jax.shard_map(local, mesh=mesh, in_specs=in_specs, out_specs=out_specs, check_vma=False)
```

```python
import functools
import math

import jax
import jax.numpy as jnp
from jax import lax
from jax.experimental import pallas as pl
from jax.experimental.pallas import tpu as pltpu
from jax.sharding import PartitionSpec as P

HEAD = 128
MASKED = -1e30
EPSILON = 1e-06
MESH = pl.DeviceIdType.MESH
ORDERS = ((0, 1, 2), (1, 2, 0), (2, 0, 1))
STRIDES = (32, 8, 2)
DEC = 4
STRETCH = 60
GROUP = 8


def dot_t(a, b):
    return lax.dot_general(a, b, (((1,), (1,)), ((), ())), preferred_element_type=jnp.float32)


def dot_n(a, b):
    return lax.dot_general(a, b, (((1,), (0,)), ((), ())), preferred_element_type=jnp.float32)


class Gather:
    def __init__(self, me, sources, buffers, send_sem, recv_sem, local_sem):
        self.me = me
        self.coords = (me // 32, (me // 8) % 4, (me // 2) % 4)
        self.core = me % 2
        self.sources, self.buffers = sources, buffers
        self.send_sem, self.recv_sem, self.local_sem = send_sem, recv_sem, local_sem
        self.started = []

    def slot(self, buffer, gathered):
        index = tuple(
            slice(None) if axis in gathered else self.coords[axis] for axis in range(3)
        )
        return buffer.at[index + (self.core,)]

    def start(self, phase):
        started = []
        for p, (source, buffer) in enumerate(zip(self.sources, self.buffers)):
            order = ORDERS[p]
            if phase == 0:
                own = pltpu.make_async_copy(source, self.slot(buffer, ()), self.local_sem.at[p])
                own.start()
                started.append(own)
            if phase < 3:
                here = self.slot(buffer, order[:phase])
                axis = order[phase]
                for d in range(1, 4):
                    peer = self.me + ((self.coords[axis] + d) % 4 - self.coords[axis]) * STRIDES[axis]
                    copy = pltpu.make_async_remote_copy(
                        src_ref=source if phase == 0 else here,
                        dst_ref=here,
                        send_sem=self.send_sem.at[p, phase * 3 + d - 1],
                        recv_sem=self.recv_sem.at[p, phase * 3 + d - 1],
                        device_id=(peer,),
                        device_id_type=MESH,
                    )
                    copy.start()
                    started.append(copy)
            else:
                here = self.slot(buffer, (0, 1, 2))
                copy = pltpu.make_async_remote_copy(
                    src_ref=here,
                    dst_ref=here,
                    send_sem=self.send_sem.at[p, 9],
                    recv_sem=self.recv_sem.at[p, 9],
                    device_id=(self.me + 1 - 2 * self.core,),
                    device_id_type=MESH,
                )
                copy.start()
                started.append(copy)
        self.started = started

    def finish(self):
        for copy in self.started:
            copy.wait()
        self.started = []


def attention_kernel(
    request_ref, place_ref, len_ref, prior_ref, q_ref, kv_ref, res_ref, gain_ref,
    routes_ref, weight_ref, prefix_hbm, cache_hbm, wout_hbm,
    hidden_ref, normed_ref, picks_ref, mix_ref,
    prefix, cache, wout, att, a0, a1, a2, b0, b1, s0, s1, q0_ref, q1_ref, pair_ref,
    load_sem, send_a, recv_a, local_a, send_b, recv_b, local_b,
):
    me = lax.axis_index("dp")
    loads = [
        pltpu.make_async_copy(prefix_hbm, prefix, load_sem.at[0]),
        pltpu.make_async_copy(cache_hbm, cache, load_sem.at[1]),
        pltpu.make_async_copy(wout_hbm, wout, load_sem.at[2]),
    ]
    for copy in loads:
        copy.start()
    first = Gather(me, (q0_ref, q1_ref, pair_ref), (a0, a1, a2), send_a, recv_a, local_a)
    second = Gather(me, (s0, s1), (b0, b1), send_b, recv_b, local_b)
    barrier = pltpu.get_barrier_semaphore()
    for axis in range(3):
        for d in range(1, 4):
            peer = me + ((first.coords[axis] + d) % 4 - first.coords[axis]) * STRIDES[axis]
            pl.semaphore_signal(barrier, inc=1, device_id=(peer,), device_id_type=MESH)
    pl.semaphore_signal(
        barrier, inc=1, device_id=(me + 1 - 2 * first.core,), device_id_type=MESH
    )
    last = q_ref[q_ref.shape[0] - 16:, :].astype(jnp.float32)
    keys = kv_ref[0, kv_ref.shape[1] - 16:, :].astype(jnp.float32)
    values = kv_ref[1, kv_ref.shape[1] - 16:, :].astype(jnp.float32)
    for s in range(DEC):
        row = slice(16 - DEC + s, 17 - DEC + s)
        for g, target in enumerate((q0_ref, q1_ref)):
            heads = [last[row, h * HEAD:(h + 1) * HEAD] for h in range(g * GROUP, (g + 1) * GROUP)]
            target[s] = jnp.concatenate(heads, axis=0).astype(jnp.bfloat16)
        parts = [plane[row, g * HEAD:(g + 1) * HEAD] for plane in (keys, values) for g in range(2)]
        pair_ref[s] = jnp.concatenate(parts, axis=0).astype(jnp.bfloat16)
    pl.semaphore_wait(barrier, 10)
    scale = 1.0 / math.sqrt(HEAD)
    rows = q_ref.shape[0]
    cache_rows = prefix.shape[2 - 1]

    def prefill(part):
        g, half = part // 2, part % 2
        heads = [g * GROUP + half * 4 + j for j in range(4)]
        q = jnp.concatenate([q_ref[:, h * HEAD:(h + 1) * HEAD] for h in heads], axis=0)
        cols = slice(g * HEAD, (g + 1) * HEAD)
        old = dot_t(q, prefix[0, :, cols]) * scale
        new = dot_t(q, kv_ref[0, :, cols]) * scale
        position = lax.broadcasted_iota(jnp.int32, old.shape, 1)
        old = jnp.where(position < prior_ref[0], old, MASKED)
        row = lax.broadcasted_iota(jnp.int32, new.shape, 0) % rows
        new = jnp.where(lax.broadcasted_iota(jnp.int32, new.shape, 1) <= row, new, MASKED)
        top = jnp.maximum(old.max(axis=-1, keepdims=True), new.max(axis=-1, keepdims=True))
        old, new = jnp.exp(old - top), jnp.exp(new - top)
        inv = 1.0 / (old.sum(axis=-1, keepdims=True) + new.sum(axis=-1, keepdims=True))
        out = dot_n((old * inv).astype(jnp.bfloat16), prefix[1, :, cols])
        out += dot_n((new * inv).astype(jnp.bfloat16), kv_ref[1, :, cols])
        for j, h in enumerate(heads):
            att[:, h * HEAD:(h + 1) * HEAD] = out[j * rows:(j + 1) * rows]

    def routing():
        tokens = routes_ref.shape[1]
        experts = picks_ref.shape[0] // GROUP
        number = lax.broadcasted_iota(jnp.int32, (experts, tokens), 0)
        dx, dy, dc = number & 3, (number >> 2) & 3, (number >> 4) & 1
        dz = (dx + dy + (number >> 5)) & 3
        expert = (
            (((me // 32 + dz) & 3) << 5)
            + ((((me // 8) % 4 + dy) & 3) << 3)
            + ((((me // 2) % 4 + dx) & 3) << 1)
            + ((me % 2 + dc) & 1)
        )
        member = jnp.zeros((experts, tokens), jnp.float32)
        weight = jnp.zeros((experts, tokens), jnp.float32)
        for k in range(routes_ref.shape[0]):
            named = routes_ref[k:k + 1, :] == expert
            member = jnp.where(named, 1.0, member)
            weight = jnp.where(named, weight_ref[k:k + 1, :], weight)
        one = lax.broadcasted_iota(jnp.int32, (tokens, tokens), 0)
        two = lax.broadcasted_iota(jnp.int32, (tokens, tokens), 1)
        earlier = jnp.where(one < two, 1.0, 0.0).astype(jnp.bfloat16)
        same = jnp.where(one == two, 1.0, 0.0).astype(jnp.bfloat16)
        rank = dot_n(member.astype(jnp.bfloat16), earlier)
        rank = jnp.where(member > 0.5, rank, -1.0).astype(jnp.bfloat16)
        high = weight.astype(jnp.bfloat16)
        rest = (weight - high.astype(jnp.float32)).astype(jnp.bfloat16)
        slots = picks_ref.shape[0]
        down = lax.broadcasted_iota(jnp.int32, (slots, experts), 0) >> 3
        spread = jnp.where(
            down == lax.broadcasted_iota(jnp.int32, (slots, experts), 1), 1.0, 0.0
        ).astype(jnp.bfloat16)
        wanted = (lax.broadcasted_iota(jnp.int32, (slots, tokens), 0) & 7).astype(jnp.float32)
        picks_ref[...] = jnp.where(dot_n(spread, rank) == wanted, 1.0, 0.0).astype(jnp.bfloat16)
        wanted = (lax.broadcasted_iota(jnp.int32, (tokens, slots), 1) & 7).astype(jnp.float32)
        turned = dot_t(same, rank).astype(jnp.bfloat16)
        chosen = dot_t(turned, spread) == wanted
        for n, table in enumerate((high, rest)):
            turned = dot_t(same, table).astype(jnp.bfloat16)
            mix_ref[n * tokens:(n + 1) * tokens, :] = jnp.where(
                chosen, dot_t(turned, spread), 0.0
            ).astype(jnp.bfloat16)

    first.start(0)
    first.finish()
    first.start(1)
    loads[0].wait()
    prefill(0)
    first.finish()
    first.start(2)
    prefill(1)
    prefill(2)
    first.finish()
    first.start(3)
    loads[1].wait()
    routing()
    first.finish()

    for s in range(DEC):
        src = request_ref[s]
        sz, sy, sx, sc = src // 128, (src // 32) % 4, (src // 8) % 4, (src // 4) % 2
        sr = src % 4
        pair = a2[sz, sy, sx, sc, sr].astype(jnp.float32)
        for g, (buf, out_ref) in enumerate(((a0, s0), (a1, s1))):
            q = buf[sz, sy, sx, sc, sr]
            cols = slice(g * HEAD, (g + 1) * HEAD)
            old = dot_t(q, cache[0, s, :, cols]) * scale
            new = (q.astype(jnp.float32) * pair[g:g + 1]).sum(axis=-1, keepdims=True) * scale
            position = lax.broadcasted_iota(jnp.int32, old.shape, 1)
            old = jnp.where(position < len_ref[s], old, MASKED)
            top = jnp.maximum(old.max(axis=-1, keepdims=True), new)
            old, new = jnp.exp(old - top), jnp.exp(new - top)
            inv = 1.0 / (old.sum(axis=-1, keepdims=True) + new)
            out = dot_n((old * inv).astype(jnp.bfloat16), cache[1, s, :, cols])
            own = (new * inv).astype(jnp.bfloat16).astype(jnp.float32)
            out_ref[s] = (out + own * pair[2 + g:3 + g]).astype(jnp.bfloat16)

    second.start(0)
    second.finish()
    second.start(1)
    second.finish()
    second.start(2)
    prefill(3)
    loads[2].wait()
    second.finish()
    second.start(3)
    second.finish()
    for s in range(DEC):
        src = place_ref[me * DEC + s]
        sz, sy, sx, sc = src // 128, (src // 32) % 4, (src // 8) % 4, (src // 4) % 2
        sr = src % 4
        for g, buf in enumerate((b0, b1)):
            out = buf[sz, sy, sx, sc, sr].astype(jnp.float32)
            for j in range(GROUP):
                h = g * GROUP + j
                att[STRETCH + s:STRETCH + s + 1, h * HEAD:(h + 1) * HEAD] = out[j:j + 1]

    attended = att[...].astype(jnp.bfloat16)
    step = 512
    total = jnp.zeros((rows, 1), jnp.float32)
    width = wout.shape[1]
    for n in range(0, width, step):
        piece = dot_n(attended, wout[:, n:n + step])
        piece = (piece + res_ref[:, n:n + step].astype(jnp.float32)).astype(jnp.bfloat16)
        hidden_ref[:, n:n + step] = piece
        piece = piece.astype(jnp.float32)
        total += (piece * piece).sum(axis=-1, keepdims=True)
    norm = lax.rsqrt(total * (1.0 / width) + EPSILON)
    gain = gain_ref[...].astype(jnp.float32)
    for n in range(width // HEAD):
        cols = slice(n * HEAD, (n + 1) * HEAD)
        piece = hidden_ref[:, cols].astype(jnp.float32) * norm * gain[n:n + 1]
        normed_ref[:, cols] = piece.astype(jnp.bfloat16)


def attention(
    request, placement, cache_len, prefix_len, queries, new_kv, residual, gain, routes, weights,
    prefix, cache, w_out,
):
    rows, width = residual.shape
    slots = lax.axis_size("dp") * GROUP
    quarter, pair = (DEC, GROUP, HEAD), (DEC, 4, HEAD)
    vmem = pl.BlockSpec(memory_space=pltpu.VMEM)
    smem = pl.BlockSpec(memory_space=pltpu.SMEM)
    hbm = pl.BlockSpec(memory_space=pl.ANY)
    bf16 = jnp.bfloat16
    dma = pltpu.SemaphoreType.DMA
    return pl.pallas_call(
        attention_kernel,
        out_shape=[
            jax.ShapeDtypeStruct((rows, width), bf16),
            jax.ShapeDtypeStruct((rows, width), bf16),
            jax.ShapeDtypeStruct((slots, rows), bf16),
            jax.ShapeDtypeStruct((2 * rows, slots), bf16),
        ],
        in_specs=[smem] * 4 + [vmem] * 6 + [hbm] * 3,
        out_specs=[vmem] * 4,
        scratch_shapes=[
            pltpu.VMEM(prefix.shape, bf16),
            pltpu.VMEM(cache.shape, bf16),
            pltpu.VMEM(w_out.shape, bf16),
            pltpu.VMEM((rows, queries.shape[1]), jnp.float32),
            pltpu.VMEM((4, 4, 4, 2) + quarter, bf16),
            pltpu.VMEM((4, 4, 4, 2) + quarter, bf16),
            pltpu.VMEM((4, 4, 4, 2) + pair, bf16),
            pltpu.VMEM((4, 4, 4, 2) + quarter, bf16),
            pltpu.VMEM((4, 4, 4, 2) + quarter, bf16),
            pltpu.VMEM(quarter, bf16),
            pltpu.VMEM(quarter, bf16),
            pltpu.VMEM(quarter, bf16),
            pltpu.VMEM(quarter, bf16),
            pltpu.VMEM(pair, bf16),
            dma((3,)),
            dma((3, 10)), dma((3, 10)), dma((3,)),
            dma((2, 10)), dma((2, 10)), dma((2,)),
        ],
        compiler_params=pltpu.CompilerParams(
            collective_id=0, has_side_effects=True, vmem_limit_bytes=56 * 2**20
        ),
        name="attention",
    )(
        request, placement, cache_len, prefix_len, queries, new_kv, residual, gain, routes, weights,
        prefix, cache, w_out,
    )


def shifted(me, k, i, sign):
    dx, dy, dc = i % 4, (i // 4) % 4, i // 16
    dz = (dx + dy + k) % 4
    z = (me // 32 + 4 + sign * dz) % 4
    y = ((me // 8) % 4 + 4 + sign * dy) % 4
    x = ((me // 2) % 4 + 4 + sign * dx) % 4
    return z * 32 + y * 8 + x * 2 + (me + dc) % 2


def experts_kernel(
    picks_ref, mix_ref, normed_ref, gate_hbm, up_hbm, down_hbm,
    out_ref,
    gate, up, down, outgoing, arrived, served, returned,
    load_sem, local_sem, send_out, recv_out, send_back, recv_back,
):
    me = lax.axis_index("dp")
    loads = [
        pltpu.make_async_copy(source.at[0], target, load_sem.at[n])
        for n, (source, target) in enumerate(((gate_hbm, gate), (up_hbm, up), (down_hbm, down)))
    ]
    for copy in loads:
        copy.start()
    barrier = pltpu.get_barrier_semaphore()
    groups, members, capacity, width = outgoing.shape
    count = members * capacity
    low = lambda k: 1 if k == 0 else 0

    for k in range(groups):
        def greet(i, carry, k=k):
            pl.semaphore_signal(
                barrier, inc=1, device_id=(shifted(me, k, i, 1),), device_id_type=MESH
            )
            return carry

        lax.fori_loop(low(k), members, greet, 0)
    for k in range(groups):
        block = dot_n(picks_ref[k * count:(k + 1) * count], normed_ref[...])
        outgoing[k] = block.astype(jnp.bfloat16).reshape(members, capacity, width)
    pl.semaphore_wait(barrier, groups * members - 1)

    def transfer(source, target, send_sem, recv_sem, k, part, peer):
        return pltpu.make_async_remote_copy(
            src_ref=source.at[k, part], dst_ref=target.at[k, part],
            send_sem=send_sem.at[k], recv_sem=recv_sem.at[k],
            device_id=(peer,), device_id_type=MESH,
        )

    def send(source, target, send_sem, recv_sem, k, sign):
        def one(i, carry):
            transfer(
                source, target, send_sem, recv_sem, k, i, shifted(me, k, i, sign)
            ).start()
            return carry

        lax.fori_loop(low(k), members, one, 0)

    def whole(source, target, send_sem, recv_sem, k):
        part = pl.ds(low(k), members - low(k))
        return transfer(source, target, send_sem, recv_sem, k, part, shifted(me, k, 1, 1))

    out_args = (outgoing, arrived, send_out, recv_out)
    back_args = (served, returned, send_back, recv_back)
    own_out = pltpu.make_async_copy(outgoing.at[0, 0], arrived.at[0, 0], local_sem.at[0])
    own_back = pltpu.make_async_copy(served.at[0, 0], returned.at[0, 0], local_sem.at[1])
    own_out.start()
    for k in range(groups):
        send(*out_args, k, 1)
    for copy in loads:
        copy.wait()
    own_out.wait()
    for k in range(groups):
        whole(*out_args, k).wait_recv()
        rows = arrived[k].reshape(count, width)
        gate_part = dot_n(rows, gate[...])
        act = gate_part / (1.0 + jnp.exp(-gate_part)) * dot_n(rows, up[...])
        result = dot_n(act.astype(jnp.bfloat16), down[...])
        served[k] = result.astype(jnp.bfloat16).reshape(members, capacity, width)
        if k == 0:
            own_back.start()
        send(*back_args, k, -1)
    own_back.wait()
    total = None
    for k in range(groups):
        whole(*back_args, k).wait_recv()
        part = dot_n(mix_ref[:, k * count:(k + 1) * count], returned[k].reshape(count, width))
        total = part if total is None else total + part
    tokens = out_ref.shape[0]
    out_ref[...] = total[:tokens] + total[tokens:]
    for k in range(groups):
        whole(*out_args, k).wait_send()
        whole(*back_args, k).wait_send()


def routed_experts(picks, mix, normed, w_gate, w_up, w_down):
    tokens, width = normed.shape
    vmem = pl.BlockSpec(memory_space=pltpu.VMEM)
    hbm = pl.BlockSpec(memory_space=pl.ANY)
    bf16 = jnp.bfloat16
    dma = pltpu.SemaphoreType.DMA
    slots = pltpu.VMEM((4, 32, picks.shape[0] // 128, width), bf16)
    return pl.pallas_call(
        experts_kernel,
        out_shape=jax.ShapeDtypeStruct((tokens, width), jnp.float32),
        in_specs=[vmem] * 3 + [hbm] * 3,
        out_specs=vmem,
        scratch_shapes=[
            pltpu.VMEM(w_gate.shape[1:], bf16),
            pltpu.VMEM(w_up.shape[1:], bf16),
            pltpu.VMEM(w_down.shape[1:], bf16),
            slots, slots, slots, slots,
            dma((3,)), dma((2,)), dma((4,)), dma((4,)), dma((4,)), dma((4,)),
        ],
        compiler_params=pltpu.CompilerParams(
            collective_id=1, has_side_effects=True, vmem_limit_bytes=56 * 2**20
        ),
        name="experts",
    )(picks, mix, normed, w_gate, w_up, w_down)


def local(
    queries, new_kv, residual, prefix_cache, prefix_len, decode_cache, cache_len, placement,
    w_out, norm_gain, routes, route_weight, w_gate, w_up, w_down,
):
    width = residual.shape[1]
    me = lax.axis_index("dp")
    slot_ids = me * DEC + jnp.arange(DEC, dtype=jnp.int32)
    request_ids = jnp.arange(placement.shape[0], dtype=jnp.int32)
    matches = placement[None, :] == slot_ids[:, None]
    request = jnp.sum(jnp.where(matches, request_ids[None, :], 0), axis=1)
    hidden_state, normed, picks, mix = attention(
        request, placement, cache_len, prefix_len, queries, new_kv, residual,
        norm_gain.reshape(width // HEAD, HEAD), routes.T, route_weight.T,
        prefix_cache[:, 0], decode_cache, w_out,
    )
    expert_sum = routed_experts(picks, mix, normed, w_gate, w_up, w_down)
    return (hidden_state.astype(jnp.float32) + expert_sum).astype(jnp.bfloat16)


def solution(mesh):
    in_specs = (
        P("dp", None),
        P(None, "dp", None),
        P("dp", None),
        P(None, "dp", None, None),
        P("dp"),
        P(None, "dp", None, None),
        P("dp"),
        P(),
        P(),
        P(),
        P("dp", None),
        P("dp", None),
        P("dp", None, None),
        P("dp", None, None),
        P("dp", None, None),
    )
    out_specs = P("dp", None)
    return jax.shard_map(local, mesh=mesh, in_specs=in_specs, out_specs=out_specs, check_vma=False)
```

```python
import math

import jax
import jax.numpy as jnp
from jax import lax
from jax.experimental import pallas as pl
from jax.experimental.pallas import tpu as pltpu
from jax.sharding import PartitionSpec as P

HEAD = 128
MASKED = -1e30
EPSILON = 1e-06
MESH = pl.DeviceIdType.MESH
ORDERS = ((0, 1, 2), (1, 2, 0), (2, 0, 1))
STRIDES = (32, 8, 2)
DEC = 4
STRETCH = 60
GROUP = 8


def dot_t(a, b):
    return lax.dot_general(a, b, (((1,), (1,)), ((), ())), preferred_element_type=jnp.float32)


def dot_n(a, b):
    return lax.dot_general(a, b, (((1,), (0,)), ((), ())), preferred_element_type=jnp.float32)


class Gather:
    def __init__(self, me, sources, buffers, send_sem, recv_sem, local_sem):
        self.me = me
        self.coords = (me // 32, (me // 8) % 4, (me // 2) % 4)
        self.core = me % 2
        self.sources, self.buffers = sources, buffers
        self.send_sem, self.recv_sem, self.local_sem = send_sem, recv_sem, local_sem
        self.started = []

    def slot(self, buffer, gathered):
        index = tuple(
            slice(None) if axis in gathered else self.coords[axis] for axis in range(3)
        )
        return buffer.at[index + (self.core,)]

    def start(self, phase):
        started = []
        for p, (source, buffer) in enumerate(zip(self.sources, self.buffers)):
            order = ORDERS[p]
            if phase == 0:
                own = pltpu.make_async_copy(source, self.slot(buffer, ()), self.local_sem.at[p])
                own.start()
                started.append(own)
            here = self.slot(buffer, order[:phase])
            axis = order[phase]
            for d in range(1, 4):
                peer = self.me + ((self.coords[axis] + d) % 4 - self.coords[axis]) * STRIDES[axis]
                copy = pltpu.make_async_remote_copy(
                    src_ref=source if phase == 0 else here,
                    dst_ref=here,
                    send_sem=self.send_sem.at[p, phase * 3 + d - 1],
                    recv_sem=self.recv_sem.at[p, phase * 3 + d - 1],
                    device_id=(peer,),
                    device_id_type=MESH,
                )
                copy.start()
                started.append(copy)
        self.started = started

    def finish(self):
        for copy in self.started:
            copy.wait()
        self.started = []

    def forward(self, p, d):
        axis = ORDERS[p][2]
        index = [slice(None)] * 3
        index[axis] = (self.coords[axis] + 4 - d) % 4
        block = self.buffers[p].at[tuple(index) + (self.core,)]
        copy = pltpu.make_async_remote_copy(
            src_ref=block,
            dst_ref=block,
            send_sem=self.send_sem.at[p, 9 + d],
            recv_sem=self.recv_sem.at[p, 9 + d],
            device_id=(self.me + 1 - 2 * self.core,),
            device_id_type=MESH,
        )
        copy.start()
        return copy

    def start_last(self):
        self.start(2)
        self.passed = [self.forward(p, 0) for p in range(len(self.buffers))]

    def finish_last(self):
        for d in (1, 3, 2):
            for p in range(len(self.buffers)):
                self.started[p * 3 + d - 1].wait_recv()
                self.passed.append(self.forward(p, d))
        for copy in self.started:
            copy.wait_send()
        for copy in self.passed:
            copy.wait()
        self.started = []


def layer_kernel(
    request_ref, place_ref, len_ref, prior_ref, q_ref, kv_ref, res_ref, gain_ref,
    routes_ref, weight_ref, prefix_hbm, cache_hbm, wout_hbm, gate_hbm, up_hbm, down_hbm,
    out_ref,
    hidden_ref, normed_ref, picks_ref, mix_ref,
    prefix, cache, wout, att, a0, a1, a2, b0, b1, b2, s0, s1, s2, q0_ref, q1_ref, pair_ref,
    load_sem, send_a, recv_a, local_a, send_b, recv_b, local_b,
    *expert_refs,
):
    me = lax.axis_index("dp")
    loads = [
        pltpu.make_async_copy(prefix_hbm, prefix, load_sem.at[0]),
        pltpu.make_async_copy(cache_hbm, cache, load_sem.at[1]),
        pltpu.make_async_copy(wout_hbm, wout, load_sem.at[2]),
    ]
    loads += [
        pltpu.make_async_copy(source.at[0], target, load_sem.at[3 + n])
        for n, (source, target) in enumerate(zip((gate_hbm, up_hbm, down_hbm), expert_refs[:3]))
    ]
    for copy in loads:
        copy.start()
    first = Gather(me, (q0_ref, q1_ref, pair_ref), (a0, a1, a2), send_a, recv_a, local_a)
    second = Gather(me, (s0, s1, s2), (b0, b1, b2), send_b, recv_b, local_b)
    barrier = pltpu.get_barrier_semaphore()
    for axis in range(3):
        for d in range(1, 4):
            peer = me + ((first.coords[axis] + d) % 4 - first.coords[axis]) * STRIDES[axis]
            pl.semaphore_signal(barrier, inc=1, device_id=(peer,), device_id_type=MESH)
    pl.semaphore_signal(
        barrier, inc=1, device_id=(me + 1 - 2 * first.core,), device_id_type=MESH
    )
    last = q_ref[q_ref.shape[0] - 16:, :].astype(jnp.float32)
    keys = kv_ref[0, kv_ref.shape[1] - 16:, :].astype(jnp.float32)
    values = kv_ref[1, kv_ref.shape[1] - 16:, :].astype(jnp.float32)
    for s in range(DEC):
        row = slice(16 - DEC + s, 17 - DEC + s)
        for g, target in enumerate((q0_ref, q1_ref)):
            heads = [last[row, h * HEAD:(h + 1) * HEAD] for h in range(g * GROUP, (g + 1) * GROUP)]
            target[s] = jnp.concatenate(heads, axis=0).astype(jnp.bfloat16)
        parts = [plane[row, g * HEAD:(g + 1) * HEAD] for plane in (keys, values) for g in range(2)]
        pair_ref[s] = jnp.concatenate(parts, axis=0).astype(jnp.bfloat16)
    pl.semaphore_wait(barrier, 10)
    scale = 1.0 / math.sqrt(HEAD)
    rows = q_ref.shape[0]
    cache_rows = prefix.shape[2 - 1]

    def prefill(part):
        g, half = part // 2, part % 2
        heads = [g * GROUP + half * 4 + j for j in range(4)]
        q = jnp.concatenate([q_ref[:, h * HEAD:(h + 1) * HEAD] for h in heads], axis=0)
        cols = slice(g * HEAD, (g + 1) * HEAD)
        old = dot_t(q, prefix[0, :, cols]) * scale
        new = dot_t(q, kv_ref[0, :, cols]) * scale
        position = lax.broadcasted_iota(jnp.int32, old.shape, 1)
        old = jnp.where(position < prior_ref[0], old, MASKED)
        row = lax.broadcasted_iota(jnp.int32, new.shape, 0) % rows
        new = jnp.where(lax.broadcasted_iota(jnp.int32, new.shape, 1) <= row, new, MASKED)
        top = jnp.maximum(old.max(axis=-1, keepdims=True), new.max(axis=-1, keepdims=True))
        old, new = jnp.exp(old - top), jnp.exp(new - top)
        inv = 1.0 / (old.sum(axis=-1, keepdims=True) + new.sum(axis=-1, keepdims=True))
        out = dot_n((old * inv).astype(jnp.bfloat16), prefix[1, :, cols])
        out += dot_n((new * inv).astype(jnp.bfloat16), kv_ref[1, :, cols])
        for j, h in enumerate(heads):
            att[:, h * HEAD:(h + 1) * HEAD] = out[j * rows:(j + 1) * rows]

    def routing():
        tokens = routes_ref.shape[1]
        experts = picks_ref.shape[0] // GROUP
        number = lax.broadcasted_iota(jnp.int32, (experts, tokens), 0)
        dx, dy, dc = number & 3, (number >> 2) & 3, (number >> 4) & 1
        dz = (dx + dy + (number >> 5)) & 3
        expert = (
            (((me // 32 + dz) & 3) << 5)
            + ((((me // 8) % 4 + dy) & 3) << 3)
            + ((((me // 2) % 4 + dx) & 3) << 1)
            + ((me % 2 + dc) & 1)
        )
        member = jnp.zeros((experts, tokens), jnp.float32)
        weight = jnp.zeros((experts, tokens), jnp.float32)
        for k in range(routes_ref.shape[0]):
            named = routes_ref[k:k + 1, :] == expert
            member = jnp.where(named, 1.0, member)
            weight = jnp.where(named, weight_ref[k:k + 1, :], weight)
        one = lax.broadcasted_iota(jnp.int32, (tokens, tokens), 0)
        two = lax.broadcasted_iota(jnp.int32, (tokens, tokens), 1)
        earlier = jnp.where(one < two, 1.0, 0.0).astype(jnp.bfloat16)
        same = jnp.where(one == two, 1.0, 0.0).astype(jnp.bfloat16)
        rank = dot_n(member.astype(jnp.bfloat16), earlier)
        rank = jnp.where(member > 0.5, rank, -1.0).astype(jnp.bfloat16)
        high = weight.astype(jnp.bfloat16)
        rest = (weight - high.astype(jnp.float32)).astype(jnp.bfloat16)
        slots = picks_ref.shape[0]
        down = lax.broadcasted_iota(jnp.int32, (slots, experts), 0) >> 3
        spread = jnp.where(
            down == lax.broadcasted_iota(jnp.int32, (slots, experts), 1), 1.0, 0.0
        ).astype(jnp.bfloat16)
        wanted = (lax.broadcasted_iota(jnp.int32, (slots, tokens), 0) & 7).astype(jnp.float32)
        picks_ref[...] = jnp.where(dot_n(spread, rank) == wanted, 1.0, 0.0).astype(jnp.bfloat16)
        wanted = (lax.broadcasted_iota(jnp.int32, (tokens, slots), 1) & 7).astype(jnp.float32)
        turned = dot_t(same, rank).astype(jnp.bfloat16)
        chosen = dot_t(turned, spread) == wanted
        for n, table in enumerate((high, rest)):
            turned = dot_t(same, table).astype(jnp.bfloat16)
            mix_ref[n * tokens:(n + 1) * tokens, :] = jnp.where(
                chosen, dot_t(turned, spread), 0.0
            ).astype(jnp.bfloat16)

    first.start(0)
    first.finish()
    first.start(1)
    loads[0].wait()
    prefill(0)
    first.finish()
    first.start_last()
    prefill(1)
    prefill(2)
    loads[1].wait()
    first.finish_last()

    for s in range(DEC):
        src = request_ref[s]
        sz, sy, sx, sc = src // 128, (src // 32) % 4, (src // 8) % 4, (src // 4) % 2
        sr = src % 4
        pair = a2[sz, sy, sx, sc, sr].astype(jnp.float32)
        for g, (buf, target) in enumerate(((a0, s0), (a1, s1))):
            q = buf[sz, sy, sx, sc, sr]
            cols = slice(g * HEAD, (g + 1) * HEAD)
            old = dot_t(q, cache[0, s, :, cols]) * scale
            new = (q.astype(jnp.float32) * pair[g:g + 1]).sum(axis=-1, keepdims=True) * scale
            position = lax.broadcasted_iota(jnp.int32, old.shape, 1)
            old = jnp.where(position < len_ref[s], old, MASKED)
            top = jnp.maximum(old.max(axis=-1, keepdims=True), new)
            old, new = jnp.exp(old - top), jnp.exp(new - top)
            inv = 1.0 / (old.sum(axis=-1, keepdims=True) + new)
            out = dot_n((old * inv).astype(jnp.bfloat16), cache[1, s, :, cols])
            own = (new * inv).astype(jnp.bfloat16).astype(jnp.float32)
            result = (out + own * pair[2 + g:3 + g]).astype(jnp.bfloat16)
            if s < DEC - 1:
                target[s] = result
            else:
                s2[g] = result

    second.start(0)
    second.finish()
    second.start(1)
    prefill(3)
    second.finish()
    second.start_last()
    routing()
    loads[2].wait()
    second.finish_last()
    for s in range(DEC):
        src = place_ref[me * DEC + s]
        sz, sy, sx, sc = src // 128, (src // 32) % 4, (src // 8) % 4, (src // 4) % 2
        sr = src % 4
        for g, buf in enumerate((b0, b1)):
            out = buf[sz, sy, sx, sc, jnp.minimum(sr, DEC - 2)].astype(jnp.float32)
            out = jnp.where(sr < DEC - 1, out, b2[sz, sy, sx, sc, g].astype(jnp.float32))
            for j in range(GROUP):
                h = g * GROUP + j
                att[STRETCH + s:STRETCH + s + 1, h * HEAD:(h + 1) * HEAD] = out[j:j + 1]

    attended = att[...].astype(jnp.bfloat16)
    step = 512
    total = jnp.zeros((rows, 1), jnp.float32)
    width = wout.shape[1]
    for n in range(0, width, step):
        piece = dot_n(attended, wout[:, n:n + step])
        piece = (piece + res_ref[:, n:n + step].astype(jnp.float32)).astype(jnp.bfloat16)
        hidden_ref[:, n:n + step] = piece
        piece = piece.astype(jnp.float32)
        total += (piece * piece).sum(axis=-1, keepdims=True)
    norm = lax.rsqrt(total * (1.0 / width) + EPSILON)
    gain = gain_ref[...].astype(jnp.float32)
    for n in range(width // HEAD):
        cols = slice(n * HEAD, (n + 1) * HEAD)
        piece = hidden_ref[:, cols].astype(jnp.float32) * norm * gain[n:n + 1]
        normed_ref[:, cols] = piece.astype(jnp.bfloat16)

    total = experts_stage(me, picks_ref, mix_ref, normed_ref, loads[3:], *expert_refs)
    out_ref[...] = (
        hidden_ref[...].astype(jnp.float32) + total[:rows] + total[rows:]
    ).astype(jnp.bfloat16)


def shifted(me, k, i, sign):
    dx, dy, dc = i % 4, (i // 4) % 4, i // 16
    dz = (dx + dy + k) % 4
    z = (me // 32 + 4 + sign * dz) % 4
    y = ((me // 8) % 4 + 4 + sign * dy) % 4
    x = ((me // 2) % 4 + 4 + sign * dx) % 4
    return z * 32 + y * 8 + x * 2 + (me + dc) % 2


def experts_stage(
    me, picks_ref, mix_ref, normed_ref, loads,
    gate, up, down, outgoing, arrived, served, returned,
    local_sem, send_out, recv_out, send_back, recv_back,
):
    groups, members, capacity, width = outgoing.shape
    count = members * capacity
    low = lambda k: 1 if k == 0 else 0

    def transfer(source, target, send_sem, recv_sem, k, part, peer):
        return pltpu.make_async_remote_copy(
            src_ref=source.at[k, part], dst_ref=target.at[k, part],
            send_sem=send_sem.at[k], recv_sem=recv_sem.at[k],
            device_id=(peer,), device_id_type=MESH,
        )

    def send(source, target, send_sem, recv_sem, k, sign):
        def one(i, carry):
            transfer(
                source, target, send_sem, recv_sem, k, i, shifted(me, k, i, sign)
            ).start()
            return carry

        lax.fori_loop(low(k), members, one, 0)

    def whole(source, target, send_sem, recv_sem, k):
        part = pl.ds(low(k), members - low(k))
        return transfer(source, target, send_sem, recv_sem, k, part, shifted(me, k, 1, 1))

    out_args = (outgoing, arrived, send_out, recv_out)
    back_args = (served, returned, send_back, recv_back)
    own_out = pltpu.make_async_copy(outgoing.at[0, 0], arrived.at[0, 0], local_sem.at[0])
    own_back = pltpu.make_async_copy(served.at[0, 0], returned.at[0, 0], local_sem.at[1])
    for k in range(groups):
        block = dot_n(picks_ref[k * count:(k + 1) * count], normed_ref[...])
        outgoing[k] = block.astype(jnp.bfloat16).reshape(members, capacity, width)
        if k == 1:
            own_out.start()
        if k:
            send(*out_args, k - 1, 1)
    send(*out_args, groups - 1, 1)
    for copy in loads:
        copy.wait()
    own_out.wait()
    for k in range(groups):
        whole(*out_args, k).wait_recv()
        rows = arrived[k].reshape(count, width)
        gate_part = dot_n(rows, gate[...])
        act = gate_part / (1.0 + jnp.exp(-gate_part)) * dot_n(rows, up[...])
        result = dot_n(act.astype(jnp.bfloat16), down[...])
        served[k] = result.astype(jnp.bfloat16).reshape(members, capacity, width)
        if k == 0:
            own_back.start()
        send(*back_args, k, -1)
    own_back.wait()
    total = None
    for k in range(groups):
        whole(*back_args, k).wait_recv()
        part = dot_n(mix_ref[:, k * count:(k + 1) * count], returned[k].reshape(count, width))
        total = part if total is None else total + part
    for k in range(groups):
        whole(*out_args, k).wait_send()
        whole(*back_args, k).wait_send()
    return total


def layer(
    request, placement, cache_len, prefix_len, queries, new_kv, residual, gain, routes, weights,
    prefix, cache, w_out, w_gate, w_up, w_down,
):
    rows, width = residual.shape
    slots = lax.axis_size("dp") * GROUP
    quarter, pair = (DEC, GROUP, HEAD), (DEC, 4, HEAD)
    vmem = pl.BlockSpec(memory_space=pltpu.VMEM)
    smem = pl.BlockSpec(memory_space=pltpu.SMEM)
    hbm = pl.BlockSpec(memory_space=pl.ANY)
    bf16 = jnp.bfloat16
    dma = pltpu.SemaphoreType.DMA
    lane = pltpu.VMEM((4, slots // (4 * GROUP), GROUP, width), bf16)
    return pl.pallas_call(
        layer_kernel,
        out_shape=jax.ShapeDtypeStruct((rows, width), bf16),
        in_specs=[smem] * 4 + [vmem] * 6 + [hbm] * 6,
        out_specs=vmem,
        scratch_shapes=[
            pltpu.VMEM((rows, width), bf16),
            pltpu.VMEM((rows, width), bf16),
            pltpu.VMEM((slots, rows), bf16),
            pltpu.VMEM((2 * rows, slots), bf16),
            pltpu.VMEM(prefix.shape, bf16),
            pltpu.VMEM(cache.shape, bf16),
            pltpu.VMEM(w_out.shape, bf16),
            pltpu.VMEM((rows, queries.shape[1]), jnp.float32),
            pltpu.VMEM((4, 4, 4, 2) + quarter, bf16),
            pltpu.VMEM((4, 4, 4, 2) + quarter, bf16),
            pltpu.VMEM((4, 4, 4, 2) + pair, bf16),
            pltpu.VMEM((4, 4, 4, 2) + (3, GROUP, HEAD), bf16),
            pltpu.VMEM((4, 4, 4, 2) + (3, GROUP, HEAD), bf16),
            pltpu.VMEM((4, 4, 4, 2) + (2, GROUP, HEAD), bf16),
            pltpu.VMEM((3, GROUP, HEAD), bf16),
            pltpu.VMEM((3, GROUP, HEAD), bf16),
            pltpu.VMEM((2, GROUP, HEAD), bf16),
            pltpu.VMEM(quarter, bf16),
            pltpu.VMEM(quarter, bf16),
            pltpu.VMEM(pair, bf16),
            dma((6,)),
            dma((3, 13)), dma((3, 13)), dma((3,)),
            dma((3, 13)), dma((3, 13)), dma((3,)),
            pltpu.VMEM(w_gate.shape[1:], bf16),
            pltpu.VMEM(w_up.shape[1:], bf16),
            pltpu.VMEM(w_down.shape[1:], bf16),
            lane, lane, lane, lane,
            dma((2,)), dma((4,)), dma((4,)), dma((4,)), dma((4,)),
        ],
        compiler_params=pltpu.CompilerParams(
            collective_id=0, has_side_effects=True, vmem_limit_bytes=60 * 2**20
        ),
        name="layer",
    )(
        request, placement, cache_len, prefix_len, queries, new_kv, residual, gain, routes, weights,
        prefix, cache, w_out, w_gate, w_up, w_down,
    )


def local(
    queries, new_kv, residual, prefix_cache, prefix_len, decode_cache, cache_len, placement,
    w_out, norm_gain, routes, route_weight, w_gate, w_up, w_down,
):
    width = residual.shape[1]
    me = lax.axis_index("dp")
    slot_ids = me * DEC + jnp.arange(DEC, dtype=jnp.int32)
    request_ids = jnp.arange(placement.shape[0], dtype=jnp.int32)
    matches = placement[None, :] == slot_ids[:, None]
    request = jnp.sum(jnp.where(matches, request_ids[None, :], 0), axis=1)
    return layer(
        request, placement, cache_len, prefix_len, queries, new_kv, residual,
        norm_gain.reshape(width // HEAD, HEAD), routes.T, route_weight.T,
        prefix_cache[:, 0], decode_cache, w_out, w_gate, w_up, w_down,
    )


def solution(mesh):
    in_specs = (
        P("dp", None),
        P(None, "dp", None),
        P("dp", None),
        P(None, "dp", None, None),
        P("dp"),
        P(None, "dp", None, None),
        P("dp"),
        P(),
        P(),
        P(),
        P("dp", None),
        P("dp", None),
        P("dp", None, None),
        P("dp", None, None),
        P("dp", None, None),
    )
    out_specs = P("dp", None)
    return jax.shard_map(local, mesh=mesh, in_specs=in_specs, out_specs=out_specs, check_vma=False)
```

```python
import math

import jax
import jax.numpy as jnp
from jax import lax
from jax.experimental import pallas as pl
from jax.experimental.pallas import tpu as pltpu
from jax.sharding import PartitionSpec as P

HEAD = 128
MASKED = -1e30
EPSILON = 1e-06
MESH = pl.DeviceIdType.MESH
ORDERS = ((0, 1, 2), (1, 2, 0), (2, 0, 1))
STRIDES = (32, 8, 2)
DEC = 4
STRETCH = 60
GROUP = 8


def dot_t(a, b):
    return lax.dot_general(a, b, (((1,), (1,)), ((), ())), preferred_element_type=jnp.float32)


def dot_n(a, b):
    return lax.dot_general(a, b, (((1,), (0,)), ((), ())), preferred_element_type=jnp.float32)


class Gather:
    def __init__(self, me, sources, buffers, send_sem, recv_sem, local_sem):
        self.me = me
        self.coords = (me // 32, (me // 8) % 4, (me // 2) % 4)
        self.core = me % 2
        self.sources, self.buffers = sources, buffers
        self.send_sem, self.recv_sem, self.local_sem = send_sem, recv_sem, local_sem
        self.started = []

    def slot(self, buffer, gathered):
        index = tuple(
            slice(None) if axis in gathered else self.coords[axis] for axis in range(3)
        )
        return buffer.at[index + (self.core,)]

    def start(self, phase):
        started = []
        for p, (source, buffer) in enumerate(zip(self.sources, self.buffers)):
            order = ORDERS[p]
            if phase == 0:
                own = pltpu.make_async_copy(source, self.slot(buffer, ()), self.local_sem.at[p])
                own.start()
                started.append(own)
            here = self.slot(buffer, order[:phase])
            axis = order[phase]
            for d in range(1, 4):
                peer = self.me + ((self.coords[axis] + d) % 4 - self.coords[axis]) * STRIDES[axis]
                copy = pltpu.make_async_remote_copy(
                    src_ref=source if phase == 0 else here,
                    dst_ref=here,
                    send_sem=self.send_sem.at[p, phase * 3 + d - 1],
                    recv_sem=self.recv_sem.at[p, phase * 3 + d - 1],
                    device_id=(peer,),
                    device_id_type=MESH,
                )
                copy.start()
                started.append(copy)
        self.started = started

    def finish(self):
        for copy in self.started:
            copy.wait()
        self.started = []

    def forward(self, p, d):
        axis = ORDERS[p][2]
        index = [slice(None)] * 3
        index[axis] = (self.coords[axis] + 4 - d) % 4
        block = self.buffers[p].at[tuple(index) + (self.core,)]
        copy = pltpu.make_async_remote_copy(
            src_ref=block,
            dst_ref=block,
            send_sem=self.send_sem.at[p, 9 + d],
            recv_sem=self.recv_sem.at[p, 9 + d],
            device_id=(self.me + 1 - 2 * self.core,),
            device_id_type=MESH,
        )
        copy.start()
        return copy

    def start_last(self):
        self.start(2)
        self.passed = [self.forward(p, 0) for p in range(len(self.buffers))]

    def finish_last(self):
        for d in (1, 3, 2):
            for p in range(len(self.buffers)):
                self.started[p * 3 + d - 1].wait_recv()
                self.passed.append(self.forward(p, d))
        for copy in self.started:
            copy.wait_send()
        for copy in self.passed:
            copy.wait()
        self.started = []


def layer_kernel(
    request_ref, place_ref, len_ref, prior_ref, q_ref, kv_ref, res_ref, gain_ref,
    routes_ref, weight_ref, prefix_hbm, cache_hbm, wout_hbm, gate_hbm, up_hbm, down_hbm,
    out_ref,
    hidden_ref, normed_ref, picks_ref, mix_ref,
    prefix, cache, wout, att, a0, a1, a2, b0, b1, b2, s0, s1, s2, q0_ref, q1_ref, pair_ref,
    load_sem, send_a, recv_a, local_a, send_b, recv_b, local_b,
    *expert_refs,
):
    me = lax.axis_index("dp")
    loads = [
        pltpu.make_async_copy(prefix_hbm, prefix, load_sem.at[0]),
        pltpu.make_async_copy(cache_hbm, cache, load_sem.at[1]),
        pltpu.make_async_copy(wout_hbm, wout, load_sem.at[2]),
    ]
    loads += [
        pltpu.make_async_copy(source.at[0], target, load_sem.at[3 + n])
        for n, (source, target) in enumerate(zip((gate_hbm, up_hbm, down_hbm), expert_refs[:3]))
    ]
    for copy in loads:
        copy.start()
    first = Gather(me, (q0_ref, q1_ref, pair_ref), (a0, a1, a2), send_a, recv_a, local_a)
    second = Gather(me, (s0, s1, s2), (b0, b1, b2), send_b, recv_b, local_b)
    barrier = pltpu.get_barrier_semaphore()
    for axis in range(3):
        for d in range(1, 4):
            peer = me + ((first.coords[axis] + d) % 4 - first.coords[axis]) * STRIDES[axis]
            pl.semaphore_signal(barrier, inc=1, device_id=(peer,), device_id_type=MESH)
    pl.semaphore_signal(
        barrier, inc=1, device_id=(me + 1 - 2 * first.core,), device_id_type=MESH
    )
    last = q_ref[q_ref.shape[0] - 16:, :].astype(jnp.float32)
    keys = kv_ref[0, kv_ref.shape[1] - 16:, :].astype(jnp.float32)
    values = kv_ref[1, kv_ref.shape[1] - 16:, :].astype(jnp.float32)
    for s in range(DEC):
        row = slice(16 - DEC + s, 17 - DEC + s)
        for g, target in enumerate((q0_ref, q1_ref)):
            heads = [last[row, h * HEAD:(h + 1) * HEAD] for h in range(g * GROUP, (g + 1) * GROUP)]
            target[s] = jnp.concatenate(heads, axis=0).astype(jnp.bfloat16)
        parts = [plane[row, g * HEAD:(g + 1) * HEAD] for plane in (keys, values) for g in range(2)]
        pair_ref[s] = jnp.concatenate(parts, axis=0).astype(jnp.bfloat16)
    pl.semaphore_wait(barrier, 10)
    scale = 1.0 / math.sqrt(HEAD)
    rows = q_ref.shape[0]
    cache_rows = prefix.shape[2 - 1]

    def prefill(part):
        g, half = part // 2, part % 2
        heads = [g * GROUP + half * 4 + j for j in range(4)]
        q = jnp.concatenate([q_ref[:, h * HEAD:(h + 1) * HEAD] for h in heads], axis=0)
        cols = slice(g * HEAD, (g + 1) * HEAD)
        old = dot_t(q, prefix[0, :, cols]) * scale
        new = dot_t(q, kv_ref[0, :, cols]) * scale
        position = lax.broadcasted_iota(jnp.int32, old.shape, 1)
        old = jnp.where(position < prior_ref[0], old, MASKED)
        row = lax.broadcasted_iota(jnp.int32, new.shape, 0) % rows
        new = jnp.where(lax.broadcasted_iota(jnp.int32, new.shape, 1) <= row, new, MASKED)
        top = jnp.maximum(old.max(axis=-1, keepdims=True), new.max(axis=-1, keepdims=True))
        old, new = jnp.exp(old - top), jnp.exp(new - top)
        inv = 1.0 / (old.sum(axis=-1, keepdims=True) + new.sum(axis=-1, keepdims=True))
        out = dot_n((old * inv).astype(jnp.bfloat16), prefix[1, :, cols])
        out += dot_n((new * inv).astype(jnp.bfloat16), kv_ref[1, :, cols])
        for j, h in enumerate(heads):
            att[:, h * HEAD:(h + 1) * HEAD] = out[j * rows:(j + 1) * rows]

    def routing():
        tokens = routes_ref.shape[1]
        experts = picks_ref.shape[0] // GROUP
        number = lax.broadcasted_iota(jnp.int32, (experts, tokens), 0)
        dx, dy, dc = number & 3, (number >> 2) & 3, (number >> 4) & 1
        dz = (dx + dy + (number >> 5)) & 3
        expert = (
            (((me // 32 + dz) & 3) << 5)
            + ((((me // 8) % 4 + dy) & 3) << 3)
            + ((((me // 2) % 4 + dx) & 3) << 1)
            + ((me % 2 + dc) & 1)
        )
        member = jnp.zeros((experts, tokens), jnp.float32)
        weight = jnp.zeros((experts, tokens), jnp.float32)
        for k in range(routes_ref.shape[0]):
            named = routes_ref[k:k + 1, :] == expert
            member = jnp.where(named, 1.0, member)
            weight = jnp.where(named, weight_ref[k:k + 1, :], weight)
        one = lax.broadcasted_iota(jnp.int32, (tokens, tokens), 0)
        two = lax.broadcasted_iota(jnp.int32, (tokens, tokens), 1)
        earlier = jnp.where(one < two, 1.0, 0.0).astype(jnp.bfloat16)
        same = jnp.where(one == two, 1.0, 0.0).astype(jnp.bfloat16)
        rank = dot_n(member.astype(jnp.bfloat16), earlier)
        rank = jnp.where(member > 0.5, rank, -1.0).astype(jnp.bfloat16)
        high = weight.astype(jnp.bfloat16)
        rest = (weight - high.astype(jnp.float32)).astype(jnp.bfloat16)
        slots = picks_ref.shape[0]
        down = lax.broadcasted_iota(jnp.int32, (slots, experts), 0) >> 3
        spread = jnp.where(
            down == lax.broadcasted_iota(jnp.int32, (slots, experts), 1), 1.0, 0.0
        ).astype(jnp.bfloat16)
        wanted = (lax.broadcasted_iota(jnp.int32, (slots, tokens), 0) & 7).astype(jnp.float32)
        picks_ref[...] = jnp.where(dot_n(spread, rank) == wanted, 1.0, 0.0).astype(jnp.bfloat16)
        wanted = (lax.broadcasted_iota(jnp.int32, (tokens, slots), 1) & 7).astype(jnp.float32)
        turned = dot_t(same, rank).astype(jnp.bfloat16)
        chosen = dot_t(turned, spread) == wanted
        for n, table in enumerate((high, rest)):
            turned = dot_t(same, table).astype(jnp.bfloat16)
            mix_ref[n * tokens:(n + 1) * tokens, :] = jnp.where(
                chosen, dot_t(turned, spread), 0.0
            ).astype(jnp.bfloat16)

    first.start(0)
    loads[0].wait()
    prefill(0)
    first.finish()
    first.start(1)
    prefill(1)
    first.finish()
    first.start_last()
    prefill(2)
    loads[1].wait()
    first.finish_last()

    olds, news, pairs = [], [], []
    for s in range(DEC):
        src = request_ref[s]
        sz, sy, sx, sc = src // 128, (src // 32) % 4, (src // 8) % 4, (src // 4) % 2
        sr = src % 4
        pairs.append(a2[sz, sy, sx, sc, sr].astype(jnp.float32))
        for g, buf in enumerate((a0, a1)):
            q = buf[sz, sy, sx, sc, sr]
            old = dot_t(q, cache[0, s, :, g * HEAD:(g + 1) * HEAD]) * scale
            position = lax.broadcasted_iota(jnp.int32, old.shape, 1)
            olds.append(jnp.where(position < len_ref[s], old, MASKED))
            own = q.astype(jnp.float32) * pairs[s][g:g + 1]
            news.append(own.sum(axis=-1, keepdims=True) * scale)
    old, new = jnp.concatenate(olds, axis=0), jnp.concatenate(news, axis=0)
    top = jnp.maximum(old.max(axis=-1, keepdims=True), new)
    old, new = jnp.exp(old - top), jnp.exp(new - top)
    inv = 1.0 / (old.sum(axis=-1, keepdims=True) + new)
    old = old * inv
    new = (new * inv).astype(jnp.bfloat16).astype(jnp.float32)
    for s in range(DEC):
        for g, target in enumerate((s0, s1)):
            part = slice((s * 2 + g) * GROUP, (s * 2 + g + 1) * GROUP)
            cols = slice(g * HEAD, (g + 1) * HEAD)
            out = dot_n(old[part].astype(jnp.bfloat16), cache[1, s, :, cols])
            result = (out + new[part] * pairs[s][2 + g:3 + g]).astype(jnp.bfloat16)
            if s < DEC - 1:
                target[s] = result
            else:
                s2[g] = result

    second.start(0)
    routing()
    second.finish()
    second.start(1)
    prefill(3)
    second.finish()
    second.start_last()
    loads[2].wait()
    second.finish_last()
    for s in range(DEC):
        src = place_ref[me * DEC + s]
        sz, sy, sx, sc = src // 128, (src // 32) % 4, (src // 8) % 4, (src // 4) % 2
        sr = src % 4
        for g, buf in enumerate((b0, b1)):
            out = buf[sz, sy, sx, sc, jnp.minimum(sr, DEC - 2)].astype(jnp.float32)
            out = jnp.where(sr < DEC - 1, out, b2[sz, sy, sx, sc, g].astype(jnp.float32))
            for j in range(GROUP):
                h = g * GROUP + j
                att[STRETCH + s:STRETCH + s + 1, h * HEAD:(h + 1) * HEAD] = out[j:j + 1]

    attended = att[...].astype(jnp.bfloat16)
    step = 512
    total = jnp.zeros((rows, 1), jnp.float32)
    width = wout.shape[1]
    for n in range(0, width, step):
        piece = dot_n(attended, wout[:, n:n + step])
        piece = (piece + res_ref[:, n:n + step].astype(jnp.float32)).astype(jnp.bfloat16)
        hidden_ref[:, n:n + step] = piece
        piece = piece.astype(jnp.float32)
        total += (piece * piece).sum(axis=-1, keepdims=True)
    norm = lax.rsqrt(total * (1.0 / width) + EPSILON)
    gain = gain_ref[...].astype(jnp.float32)
    for n in range(width // HEAD):
        cols = slice(n * HEAD, (n + 1) * HEAD)
        piece = hidden_ref[:, cols].astype(jnp.float32) * norm * gain[n:n + 1]
        normed_ref[:, cols] = piece.astype(jnp.bfloat16)

    total = experts_stage(me, picks_ref, mix_ref, normed_ref, loads[3:], *expert_refs)
    out_ref[...] = (
        hidden_ref[...].astype(jnp.float32) + total[:rows] + total[rows:]
    ).astype(jnp.bfloat16)


def shifted(me, k, i, sign):
    dx, dy, dc = i % 4, (i // 4) % 4, i // 16
    dz = (dx + dy + k) % 4
    z = (me // 32 + 4 + sign * dz) % 4
    y = ((me // 8) % 4 + 4 + sign * dy) % 4
    x = ((me // 2) % 4 + 4 + sign * dx) % 4
    return z * 32 + y * 8 + x * 2 + (me + dc) % 2


def experts_stage(
    me, picks_ref, mix_ref, normed_ref, loads,
    gate, up, down, outgoing, arrived, served, returned,
    local_sem, send_out, recv_out, send_back, recv_back,
):
    groups, members, capacity, width = outgoing.shape
    count = members * capacity
    low = lambda k: 1 if k == 0 else 0

    def transfer(source, target, send_sem, recv_sem, k, part, peer):
        return pltpu.make_async_remote_copy(
            src_ref=source.at[k, part], dst_ref=target.at[k, part],
            send_sem=send_sem.at[k], recv_sem=recv_sem.at[k],
            device_id=(peer,), device_id_type=MESH,
        )

    def send(source, target, send_sem, recv_sem, k, sign):
        def one(i, carry):
            transfer(
                source, target, send_sem, recv_sem, k, i, shifted(me, k, i, sign)
            ).start()
            return carry

        lax.fori_loop(low(k), members, one, 0)

    def whole(source, target, send_sem, recv_sem, k):
        part = pl.ds(low(k), members - low(k))
        return transfer(source, target, send_sem, recv_sem, k, part, shifted(me, k, 1, 1))

    out_args = (outgoing, arrived, send_out, recv_out)
    back_args = (served, returned, send_back, recv_back)
    own_out = pltpu.make_async_copy(outgoing.at[0, 0], arrived.at[0, 0], local_sem.at[0])
    own_back = pltpu.make_async_copy(served.at[0, 0], returned.at[0, 0], local_sem.at[1])
    for k in range(groups):
        block = dot_n(picks_ref[k * count:(k + 1) * count], normed_ref[...])
        outgoing[k] = block.astype(jnp.bfloat16).reshape(members, capacity, width)
        if k == 1:
            own_out.start()
        if k:
            send(*out_args, k - 1, 1)
    send(*out_args, groups - 1, 1)
    for copy in loads:
        copy.wait()
    own_out.wait()
    for k in range(groups):
        whole(*out_args, k).wait_recv()
        rows = arrived[k].reshape(count, width)
        gate_part = dot_n(rows, gate[...])
        act = gate_part / (1.0 + jnp.exp(-gate_part)) * dot_n(rows, up[...])
        result = dot_n(act.astype(jnp.bfloat16), down[...])
        served[k] = result.astype(jnp.bfloat16).reshape(members, capacity, width)
        if k == 0:
            own_back.start()
        send(*back_args, k, -1)
    own_back.wait()
    total = None
    for k in range(groups):
        whole(*back_args, k).wait_recv()
        part = dot_n(mix_ref[:, k * count:(k + 1) * count], returned[k].reshape(count, width))
        total = part if total is None else total + part
    for k in range(groups):
        whole(*out_args, k).wait_send()
        whole(*back_args, k).wait_send()
    return total


def layer(
    request, placement, cache_len, prefix_len, queries, new_kv, residual, gain, routes, weights,
    prefix, cache, w_out, w_gate, w_up, w_down,
):
    rows, width = residual.shape
    slots = lax.axis_size("dp") * GROUP
    quarter, pair = (DEC, GROUP, HEAD), (DEC, 4, HEAD)
    vmem = pl.BlockSpec(memory_space=pltpu.VMEM)
    smem = pl.BlockSpec(memory_space=pltpu.SMEM)
    hbm = pl.BlockSpec(memory_space=pl.ANY)
    bf16 = jnp.bfloat16
    dma = pltpu.SemaphoreType.DMA
    lane = pltpu.VMEM((4, slots // (4 * GROUP), GROUP, width), bf16)
    return pl.pallas_call(
        layer_kernel,
        out_shape=jax.ShapeDtypeStruct((rows, width), bf16),
        in_specs=[smem] * 4 + [vmem] * 6 + [hbm] * 6,
        out_specs=vmem,
        scratch_shapes=[
            pltpu.VMEM((rows, width), bf16),
            pltpu.VMEM((rows, width), bf16),
            pltpu.VMEM((slots, rows), bf16),
            pltpu.VMEM((2 * rows, slots), bf16),
            pltpu.VMEM(prefix.shape, bf16),
            pltpu.VMEM(cache.shape, bf16),
            pltpu.VMEM(w_out.shape, bf16),
            pltpu.VMEM((rows, queries.shape[1]), jnp.float32),
            pltpu.VMEM((4, 4, 4, 2) + quarter, bf16),
            pltpu.VMEM((4, 4, 4, 2) + quarter, bf16),
            pltpu.VMEM((4, 4, 4, 2) + pair, bf16),
            pltpu.VMEM((4, 4, 4, 2) + (3, GROUP, HEAD), bf16),
            pltpu.VMEM((4, 4, 4, 2) + (3, GROUP, HEAD), bf16),
            pltpu.VMEM((4, 4, 4, 2) + (2, GROUP, HEAD), bf16),
            pltpu.VMEM((3, GROUP, HEAD), bf16),
            pltpu.VMEM((3, GROUP, HEAD), bf16),
            pltpu.VMEM((2, GROUP, HEAD), bf16),
            pltpu.VMEM(quarter, bf16),
            pltpu.VMEM(quarter, bf16),
            pltpu.VMEM(pair, bf16),
            dma((6,)),
            dma((3, 13)), dma((3, 13)), dma((3,)),
            dma((3, 13)), dma((3, 13)), dma((3,)),
            pltpu.VMEM(w_gate.shape[1:], bf16),
            pltpu.VMEM(w_up.shape[1:], bf16),
            pltpu.VMEM(w_down.shape[1:], bf16),
            lane, lane, lane, lane,
            dma((2,)), dma((4,)), dma((4,)), dma((4,)), dma((4,)),
        ],
        compiler_params=pltpu.CompilerParams(
            collective_id=0, has_side_effects=True, vmem_limit_bytes=60 * 2**20
        ),
        name="layer",
    )(
        request, placement, cache_len, prefix_len, queries, new_kv, residual, gain, routes, weights,
        prefix, cache, w_out, w_gate, w_up, w_down,
    )


def local(
    queries, new_kv, residual, prefix_cache, prefix_len, decode_cache, cache_len, placement,
    w_out, norm_gain, routes, route_weight, w_gate, w_up, w_down,
):
    width = residual.shape[1]
    me = lax.axis_index("dp")
    slot_ids = me * DEC + jnp.arange(DEC, dtype=jnp.int32)
    request_ids = jnp.arange(placement.shape[0], dtype=jnp.int32)
    matches = placement[None, :] == slot_ids[:, None]
    request = jnp.sum(jnp.where(matches, request_ids[None, :], 0), axis=1)
    return layer(
        request, placement, cache_len, prefix_len, queries, new_kv, residual,
        norm_gain.reshape(width // HEAD, HEAD), routes.T, route_weight.T,
        prefix_cache[:, 0], decode_cache, w_out, w_gate, w_up, w_down,
    )


def solution(mesh):
    in_specs = (
        P("dp", None),
        P(None, "dp", None),
        P("dp", None),
        P(None, "dp", None, None),
        P("dp"),
        P(None, "dp", None, None),
        P("dp"),
        P(),
        P(),
        P(),
        P("dp", None),
        P("dp", None),
        P("dp", None, None),
        P("dp", None, None),
        P("dp", None, None),
    )
    out_specs = P("dp", None)
    return jax.shard_map(local, mesh=mesh, in_specs=in_specs, out_specs=out_specs, check_vma=False)
```
